32 devices in a mesh: tmpl: 2 (over y), freq: 16 (over z, x, core).
Axes of the slice: x: 2, y: 2, z: 4, core: 2. Of those that a mesh axis runs over, the one named last changes fastest.
Arguments:
- strain: bfloat16 [3, 1024, 512], P(None, 'freq'), may hold values from -6 to 6
- gate_start: int32 [3, 2], replicated, may hold values from 0 to 520191
- psd_inverse: float32 [3, 512, 1024], P(None, 'freq'), may hold values from 0.5 to 6, as said below
- templates: bfloat16 [8, 2, 512, 1024], P('tmpl', None, 'freq'), may hold values from -6 to 6
- basis: bfloat16 [3, 4, 512, 1024], P(None, None, 'freq'), may hold values from -2.5 to 4.5
Outputs:
- best: float32 [512, 1024], P('tmpl', 'freq')
The draws below stay inside these ranges and needn't reach their ends.
Inputs may be any that keep to these rules, and one draw needn't show every extreme that they name: `psd_inverse`: positive weights.
All inputs are finite; a program needn't handle non-finite values.
Results may differ from the reference program's by a relative error of at most 0.004.
Values may be sent and summed in bfloat16 or wider, within the bound.
No kernel may reach another device: no remote copies, remote signals or barrier semaphores. Data moves between devices by JAX's collectives and lax.ppermute only.
A program may use at most 128 MiB of HBM per device.

```python
import math
import jax
import jax.numpy as jnp
from jax import lax

N1 = 512
N2 = 1024
DET = 3
CAL = 4
RESP = 5
TEMPLATES = 8
GATES = 2
GATE_LEN = 4096


def draw_psd_inverse(key, part):
    base = jnp.exp(jax.random.uniform(key, (DET, N1, N2), jnp.float32, math.log(0.5), math.log(2.0)))
    fraction = jnp.arange(N1, dtype=jnp.float32) / (N1 - 1)
    ramp = jnp.sqrt(1.0 + 2.0 * fraction)
    return base * ramp[None, :, None]


def draw_basis(key, part):
    key_level = jax.random.fold_in(key, 11)
    key_noise = jax.random.fold_in(key, 23)
    level = jax.random.uniform(key_level, (DET, CAL, 1, 1), jnp.float32, 0.5, 1.5)
    noise = jnp.clip(0.7 * jax.random.normal(key_noise, (DET, CAL, N1, N2), jnp.float32), -2.8, 2.8)
    return (level + noise).astype(jnp.bfloat16)


def touch_ends(result, rng, low, top_value):
    extent = result.shape
    place = [jax.random.randint(jax.random.fold_in(rng, axis), (), 0, extent[axis]) for axis in range(len(extent))]
    result = result.at[tuple(place)].set(low)
    longest = extent.index(max(extent))
    place[longest] = (place[longest] + 1) % extent[longest]
    return result.at[tuple(place)].set(top_value)


def level_of(stream_key, dims, split, smallest, top_value):
    def one(position, parts):
        heights = jax.random.uniform(jax.random.fold_in(jax.random.fold_in(stream_key, 6), position), (parts,), jnp.float32, smallest / len(split), top_value / len(split))
        return jnp.repeat(jnp.exp(heights), dims[position] // parts).reshape((-1,) + (1,) * (len(dims) - position - 1))

    gain = one(*split[0])
    for cut in split[1:]:
        gain = gain * one(*cut)
    return gain


def gaussian(own_key, shape, width, limit, pieces=(), kind=jnp.bfloat16):
    level = level_of(own_key, shape, pieces, -0.22, 0.18) if pieces else 1.0
    result = jax.random.normal(own_key, shape, jnp.float32) * width * level
    return jnp.minimum(jnp.maximum(result, -limit), limit).astype(kind)


def setup_inputs(seed: int = 0) -> dict:
    keys = jax.random.split(jax.random.key(seed), 6)
    return {
        "strain": gaussian(keys[0], (DET, N2, N1), 1.0, 6.0, ((1, 16),)),
        "gate_start": touch_ends(jax.random.randint(keys[1], (DET, GATES), 0, N1 * N2 - GATE_LEN), jax.random.fold_in(keys[1], 1), 0, (N1 * N2 - GATE_LEN) - 1).astype(jnp.int32),
        "psd_inverse": draw_psd_inverse(jax.random.fold_in(keys[5], 71), 0),
        "templates": gaussian(keys[3], (TEMPLATES, 2, N1, N2), 1.0, 6.0, ((0, 2), (2, 16))),
        "basis": draw_basis(jax.random.fold_in(keys[5], 71), 0),
    }


def fourier_table(length, orient):
    indices = jnp.arange(length, dtype=jnp.int32)
    products = (indices[:, None] * indices[None, :]) % length
    angles = products.astype(jnp.float32) * (2.0 * math.pi / length)
    return jnp.cos(angles), orient * jnp.sin(angles)


def real_table(length):
    cosines, sine_part = fourier_table(length, -1.0)
    return jnp.concatenate([cosines, sine_part], axis=1).astype(jnp.bfloat16)


def complex_table(length, orient):
    cosines, sine_part = fourier_table(length, orient)
    upper_row = jnp.concatenate([cosines, sine_part], axis=1)
    bottom = jnp.concatenate([-sine_part, cosines], axis=1)
    return jnp.stack([upper_row, bottom], axis=0).astype(jnp.bfloat16)


def twiddle_table(row_index, col_index, modulus, orient):
    products = (row_index[:, None] * col_index[None, :]) % modulus
    angles = products.astype(jnp.float32) * (2.0 * math.pi / modulus)
    return jnp.cos(angles), orient * jnp.sin(angles)


def rotate(real_part, imag_part, cosines, sine_part):
    return real_part * cosines - imag_part * sine_part, real_part * sine_part + imag_part * cosines


def statistic(real_lags, imag_lags, variance, projection, spread):
    base_real = real_lags[:, 0]
    base_imag = imag_lags[:, 0]
    head_term = (base_real * base_real + base_imag * base_imag) / ((N1 * N2) * variance[:, None, None])
    remain_real = real_lags[:, 1:] - projection[:, :, None, None] * base_real[:, None]
    remain_imag = imag_lags[:, 1:] - projection[:, :, None, None] * base_imag[:, None]
    tail_term = jnp.sum((remain_real * remain_real + remain_imag * remain_imag) / spread[:, :, None, None], axis=1)
    return jnp.sum(head_term + tail_term, axis=0) / (DET * RESP)


def reference(strain, gate_start, psd_inverse, templates, basis):
    modulus = N1 * N2
    sample = N2 * jnp.arange(N1, dtype=jnp.int32)[None, :] + jnp.arange(N2, dtype=jnp.int32)[:, None]
    starts = gate_start[:, :, None, None]
    inside = (sample[None, None] >= starts) & (sample[None, None] < starts + GATE_LEN)
    keep_mask = jnp.where(jnp.any(inside, axis=1), 0.0, 1.0).astype(jnp.bfloat16)
    gated_strain = strain * keep_mask
    section = jnp.einsum("dcn,nq->dcq", gated_strain.astype(jnp.float32), real_table(N1).astype(jnp.float32))
    section = section.reshape(DET, N2, 2, N1)
    cosines, sine_part = twiddle_table(jnp.arange(N2, dtype=jnp.int32), jnp.arange(N1, dtype=jnp.int32), modulus, -1.0)
    real_part, imag_part = rotate(section[:, :, 0], section[:, :, 1], cosines, sine_part)
    section_one = jnp.stack([real_part, imag_part], axis=2).astype(jnp.bfloat16)
    spectrum = jnp.einsum("dnpk,pnq->dkq", section_one.astype(jnp.float32), complex_table(N2, -1.0).astype(jnp.float32))
    data_real = spectrum[..., :N2] * psd_inverse
    data_imag = spectrum[..., N2:] * psd_inverse
    basis_float = basis.astype(jnp.float32)
    responses = jnp.concatenate([jnp.ones((DET, 1, N1, N2), jnp.float32), basis_float], axis=1)
    table_lag = complex_table(N2, 1.0).astype(jnp.float32)
    table_row = complex_table(N1, 1.0).astype(jnp.float32)
    back_cos, back_sin = twiddle_table(jnp.arange(N1, dtype=jnp.int32), jnp.arange(N2, dtype=jnp.int32), modulus, 1.0)

    def one_template(template):
        template_real = template[0].astype(jnp.float32)
        template_imag = template[1].astype(jnp.float32)
        product_real = data_real * template_real + data_imag * template_imag
        product_imag = data_imag * template_real - data_real * template_imag
        filtered = jnp.stack([product_real[:, None] * responses, product_imag[:, None] * responses], axis=2).astype(jnp.bfloat16)
        weight = psd_inverse * psd_inverse * (template_real * template_real + template_imag * template_imag)
        variance = jnp.sum(weight, axis=(1, 2))
        projection = jnp.einsum("dkm,djkm->dj", weight, basis_float) / variance[:, None]
        centred = basis_float - projection[:, :, None, None]
        spread = modulus * jnp.sum(weight[:, None] * centred * centred, axis=(2, 3))
        lag_section = jnp.einsum("djpkm,pmq->djkq", filtered.astype(jnp.float32), table_lag)
        lag_section = lag_section.reshape(DET, RESP, N1, 2, N2)
        real_part, imag_part = rotate(lag_section[:, :, :, 0], lag_section[:, :, :, 1], back_cos, back_sin)
        lag_one = jnp.stack([real_part, imag_part], axis=3).astype(jnp.bfloat16)
        lags = jnp.einsum("djkpn,pkq->djnq", lag_one.astype(jnp.float32), table_row)
        return statistic(lags[..., :N1], lags[..., N1:], variance, projection, spread)

    statistics = lax.map(one_template, templates)
    return jnp.max(statistics, axis=0).T
```

```python
import functools
import math

import jax
import jax.numpy as jnp
from jax import lax
from jax.experimental import pallas as pl
from jax.experimental.pallas import tpu as pltpu
from jax.sharding import PartitionSpec as P

N1 = 512
N2 = 1024
DET = 3
CAL = 4
RESP = 5
GATE_LEN = 4096
MODULUS = N1 * N2
RADIX_C = 8
RADIX_R = 4
PART = 128
HALF_ROOT = math.sqrt(0.5)


def phase(products, length):
    angles = (products % length).astype(jnp.float32) * (2.0 * math.pi / length)
    return jnp.cos(angles), jnp.sin(angles)


def times(left, right):
    return left[0] * right[0] - left[1] * right[1], left[0] * right[1] + left[1] * right[0]


def product_phase(rows, cols, length):
    fine = jnp.arange(32, dtype=jnp.int32)
    coarse = 32 * jnp.arange(rows // 32, dtype=jnp.int32)
    high = phase(coarse[:, None] * cols, length)
    low = phase(fine[:, None] * cols, length)
    real, imag = times([h[:, None] for h in high], [w[None] for w in low])
    return real.reshape(rows, -1), imag.reshape(rows, -1)


def iota(count):
    return jnp.arange(count, dtype=jnp.int32)


def forward_tables():
    cos_r, sin_r = product_phase(N1, iota(N1)[None], N1)
    table_r = jnp.concatenate([cos_r, -sin_r], axis=0).astype(jnp.bfloat16)
    cos_c, sin_c = product_phase(N2, iota(N2)[None], N2)
    upper = jnp.concatenate([cos_c, -sin_c], axis=1)
    lower = jnp.concatenate([sin_c, cos_c], axis=1)
    table_c = jnp.stack([upper, lower]).astype(jnp.bfloat16)
    twiddle = product_phase(N1, iota(N2)[None], MODULUS)
    return table_r, table_c, twiddle


def backward_tables():
    place = iota(PART)
    first = iota(RADIX_C)
    cols = first[:, None] + RADIX_C * place[None, :]
    cos_a, sin_a = phase(place[None, :, None] * cols[:, None, :], N2)
    stage_one = jnp.concatenate(
        [jnp.concatenate([cos_a, sin_a], axis=2), jnp.concatenate([-sin_a, cos_a], axis=2)], axis=1
    ).astype(jnp.bfloat16)
    rows = iota(RADIX_R)[:, None] + RADIX_R * place[None, :]
    cos_b, sin_b = phase(rows[:, :, None] * place[None, None, :], N1)
    stage_two = jnp.concatenate(
        [jnp.concatenate([cos_b, -sin_b], axis=2), jnp.concatenate([sin_b, cos_b], axis=2)], axis=1
    ).astype(jnp.bfloat16)
    fine = iota(32)
    coarse = 32 * iota(N1 // 32)
    high = phase(coarse[None, :, None] * cols[:, None, :], MODULUS)
    low = phase(fine[None, :, None] * cols[:, None, :], MODULUS)
    real, imag = times([h[:, :, None] for h in high], [w[:, None] for w in low])
    twiddle = jnp.concatenate([real, imag], axis=3).reshape(RADIX_C, N1, 2 * PART)
    order = cols.reshape(-1)
    unscramble = (order[:, None] == iota(N2)[None, :]).astype(jnp.bfloat16)
    return stage_one, stage_two, twiddle, unscramble


class Plan:
    def __init__(self, freq, templates, groups):
        self.freq, self.width, self.groups = freq, templates, groups
        self.planes = freq // templates
        self.bits = [1 << b for b in reversed(range(templates.bit_length() - 1))]
        self.offsets = [0]
        for b in self.bits:
            self.offsets = self.offsets + [o ^ b for o in self.offsets]

    def swap(self, bit):
        return [(f, f ^ bit) for f in range(self.freq)]

    def devices(self, pairs):
        w = self.width
        return [(a * w + k, b * w + k) for a, b in pairs for k in range(w)]

    def shift_in(self, o):
        n = self.planes
        return self.devices([(z, (z + o) % n) for z in range(n) if (z + o) % n < DET])

    def shift_out(self, o):
        n = self.planes
        return self.devices([(z, (z + o) % n) for z in range(DET)])

    def up(self):
        return self.devices([(z, z + 1) for z in range(DET - 1)])

    def down(self):
        return self.devices([(z + 1, z) for z in range(self.planes - 1)])

    def slot(self, k, other):
        differ = k ^ other
        return sum(((differ // b) % 2) << i for i, b in enumerate(self.bits))


def pick(array, index, axis=0):
    return lax.dynamic_index_in_dim(array, index, axis, keepdims=False)


def scatter_planes(plan, plane, array):
    got = [pick(array, jnp.minimum(plane, DET - 1))]
    for o in range(1, plan.planes):
        send = pick(array, jnp.minimum((plane + o) % plan.planes, DET - 1))
        got.append(lax.ppermute(send, "freq", plan.shift_in(o)))
    return jnp.stack(got)


def gather_plane(plan, piece):
    held = piece[None]
    pieces = [held]
    for b in plan.bits:
        got = lax.ppermute(held, "freq", plan.swap(b))
        pieces.append(got)
        held = jnp.concatenate([held, got])
    return pieces


def scatter_templates(plan, place, templates):
    held = templates[None]
    for b in plan.bits:
        mine = (place // b) % 2
        halves = held.reshape((held.shape[0], 2, held.shape[1] // 2) + held.shape[2:])
        got = lax.ppermute(pick(halves, 1 - mine, 1), "freq", plan.swap(b))
        held = jnp.concatenate([pick(halves, mine, 1), got])
    return held[:, 0]


def gather_templates(plan, piece):
    below, above = [], []
    held = piece
    for _ in range(plan.planes - 1):
        held = lax.ppermute(held, "freq", plan.down())
        above.append(held)
    held = piece
    for _ in range(DET - 1):
        held = lax.ppermute(held, "freq", plan.up())
        below.append(held)
    return below, above


def dft_eight(real, imag):
    def add(a, b):
        return real_imag[a][0] + real_imag[b][0], real_imag[a][1] + real_imag[b][1]

    def sub(a, b):
        return real_imag[a][0] - real_imag[b][0], real_imag[a][1] - real_imag[b][1]

    real_imag = list(zip(real, imag))
    a0, a1 = add(0, 4), sub(0, 4)
    a2, a3 = add(2, 6), sub(2, 6)
    a4, a5 = add(1, 5), sub(1, 5)
    a6, a7 = add(3, 7), sub(3, 7)
    e0 = (a0[0] + a2[0], a0[1] + a2[1])
    e1 = (a0[0] - a2[0], a0[1] - a2[1])
    o0 = (a4[0] + a6[0], a4[1] + a6[1])
    o1 = (a4[0] - a6[0], a4[1] - a6[1])
    f0 = (a1[0] - a3[1], a1[1] + a3[0])
    f1 = (a1[0] + a3[1], a1[1] - a3[0])
    m = (HALF_ROOT * (a5[0] - a7[0]), HALF_ROOT * (a5[1] - a7[1]))
    n = (HALF_ROOT * (a5[0] + a7[0]), HALF_ROOT * (a5[1] + a7[1]))
    g0 = (m[0] - n[1], m[1] + n[0])
    g1 = (-m[0] - n[1], n[0] - m[1])
    return [
        (e0[0] + o0[0], e0[1] + o0[1]),
        (f0[0] + g0[0], f0[1] + g0[1]),
        (e1[0] - o1[1], e1[1] + o1[0]),
        (f1[0] + g1[0], f1[1] + g1[1]),
        (e0[0] - o0[0], e0[1] - o0[1]),
        (f0[0] - g0[0], f0[1] - g0[1]),
        (e1[0] + o1[1], e1[1] - o1[0]),
        (f1[0] - g1[0], f1[1] - g1[1]),
    ]


def dft_four(real, imag):
    s0, s1 = (real[0] + real[2], imag[0] + imag[2]), (real[0] - real[2], imag[0] - imag[2])
    t0, t1 = (real[1] + real[3], imag[1] + imag[3]), (real[1] - real[3], imag[1] - imag[3])
    return [
        (s0[0] + t0[0], s0[1] + t0[1]),
        (s1[0] - t1[1], s1[1] + t1[0]),
        (s0[0] - t0[0], s0[1] - t0[1]),
        (s1[0] + t1[1], s1[1] - t1[0]),
    ]


def total(array):
    return jnp.sum(jnp.sum(array, axis=0, keepdims=True), axis=1, keepdims=True)


def lag_kernel(
    plan, rows, where_ref, spectrum, stage_one, stage_two, twiddle, unscramble, *rest
):
    n_tmpl = DET - 1 + plan.planes
    n_piece = 1 + len(plan.bits)
    tmpl_in, rest = rest[:n_tmpl], rest[n_tmpl:]
    psd_in, rest = rest[:n_piece], rest[n_piece:]
    own_in, rest = rest[:n_piece], rest[n_piece:]
    other_in, rest = rest[:n_piece], rest[n_piece:]
    out = rest[0]
    tmpl, psd, basis, prod, weight, inner, base, score, natural, acc, sem = rest[1:]
    plane, place = where_ref[0], where_ref[1]
    freq, width, planes = plan.freq, plan.width, plan.planes

    def from_plane_gather(pieces, put):
        m = 0
        for piece in pieces:
            for i in range(piece.shape[0]):
                for o in range(planes):
                    source = lax.rem(plane - o + planes, planes) * width + (place ^ plan.offsets[m])
                    put(piece.at[i, o], source)
                m += 1

    @pl.when(plane >= DET)
    def _():
        out[...] = jnp.zeros_like(out)

    @pl.when(plane < DET)
    def _():
        def copy_tmpl(ref, source_plane):
            for m in range(width):
                source = source_plane * width + (place ^ plan.offsets[m])
                pltpu.make_async_copy(ref.at[m], tmpl.at[source], sem.at[0]).start()

        copy_tmpl(tmpl_in[0], plane)
        for s in range(1, DET):
            @pl.when(plane >= s)
            def _(s=s):
                copy_tmpl(tmpl_in[s], plane - s)
        for s in range(1, planes):
            @pl.when(plane + s < planes)
            def _(s=s):
                copy_tmpl(tmpl_in[DET - 1 + s], plane + s)

        from_plane_gather(
            psd_in, lambda src, f: pltpu.make_async_copy(src.at[1], psd.at[f], sem.at[1]).start()
        )
        for j in range(2):
            from_plane_gather(
                own_in,
                lambda src, f, j=j: pltpu.make_async_copy(
                    src.at[j], basis.at[j, f], sem.at[2]
                ).start(),
            )
            from_plane_gather(
                other_in,
                lambda src, f, j=j: pltpu.make_async_copy(
                    src.at[j], basis.at[2 + j, f], sem.at[2]
                ).start(),
            )
        pltpu.make_async_copy(tmpl, tmpl, sem.at[0]).wait()
        pltpu.make_async_copy(psd, psd, sem.at[1]).wait()

        def spread_out(block, real, imag):
            tiles = [slice(a * PART, (a + 1) * PART) for a in range(RADIX_C)]
            parts = dft_eight([real[:, t] for t in tiles], [imag[:, t] for t in tiles])
            for c0, (re, im) in enumerate(parts):
                both = jnp.concatenate([re, im], axis=1)
                inner[c0, block] = both.astype(inner.dtype)

        def fold(array):
            return jnp.sum(array.reshape(rows // 8, 8, N2), axis=0)

        acc[...] = jnp.zeros_like(acc)

        def start_block(block, carry):
            at = pl.ds(pl.multiple_of(block * rows, rows), rows)
            t_re = tmpl[block, 0].astype(jnp.float32)
            t_im = tmpl[block, 1].astype(jnp.float32)
            inverse = psd[block].astype(jnp.float32)
            x_re = spectrum[at, :N2] * inverse
            x_im = spectrum[at, N2:] * inverse
            p_re = x_re * t_re + x_im * t_im
            p_im = x_im * t_re - x_re * t_im
            heavy = inverse * inverse * (t_re * t_re + t_im * t_im)
            prod[0, at] = p_re
            prod[1, at] = p_im
            weight[at] = heavy
            acc[0] += fold(heavy)
            spread_out(block, p_re, p_im)
            return carry

        lax.fori_loop(0, freq, start_block, 0)
        variance = total(acc[0])

        def transforms(use):
            def pair(cp, carry):
                columns = [[] for _ in range(RADIX_R)]
                for half in range(2):
                    c0 = 2 * cp + half
                    left = inner[c0].reshape(N1, 2 * PART).astype(jnp.bfloat16)
                    lag = jnp.dot(left, stage_one[c0], preferred_element_type=jnp.float32)
                    g_re, g_im = lag[:, :PART], lag[:, PART:]
                    tw_re, tw_im = twiddle[c0, :, :PART], twiddle[c0, :, PART:]
                    y_re = g_re * tw_re - g_im * tw_im
                    y_im = g_re * tw_im + g_im * tw_re
                    cuts = [slice(a * PART, (a + 1) * PART) for a in range(RADIX_R)]
                    parts = dft_four([y_re[t] for t in cuts], [y_im[t] for t in cuts])
                    for r0, (re, im) in enumerate(parts):
                        columns[r0].append(jnp.concatenate([re, im], axis=0).astype(jnp.bfloat16))
                for r0 in range(RADIX_R):
                    right = jnp.concatenate(columns[r0], axis=1)
                    lag = jnp.dot(stage_two[r0], right, preferred_element_type=jnp.float32)
                    use(cp, r0, lag[:PART], lag[PART:])
                return carry

            lax.fori_loop(0, RADIX_C // 2, pair, 0)

        head_scale = 1.0 / (MODULUS * variance)

        def use_base(cp, r0, re, im):
            base[cp, r0, :PART] = re
            base[cp, r0, PART:] = im
            score[cp, r0] = (re * re + im * im) * head_scale

        transforms(use_base)
        pltpu.make_async_copy(basis, basis, sem.at[2]).wait()

        def response(j, carry):
            acc[...] = jnp.zeros_like(acc)

            def filter_block(block, inside):
                at = pl.ds(pl.multiple_of(block * rows, rows), rows)
                factor = basis[j, block].astype(jnp.float32)
                acc[0] += fold(weight[at] * factor)
                spread_out(block, prod[0, at] * factor, prod[1, at] * factor)
                return inside

            lax.fori_loop(0, freq, filter_block, 0)
            projection = total(acc[0]) / variance

            def spread_block(block, inside):
                at = pl.ds(pl.multiple_of(block * rows, rows), rows)
                centred = basis[j, block].astype(jnp.float32) - projection
                acc[1] += fold(weight[at] * centred * centred)
                return inside

            lax.fori_loop(0, freq, spread_block, 0)
            tail_scale = 1.0 / (MODULUS * total(acc[1]))

            def use_tail(cp, r0, re, im):
                d_re = re - projection * base[cp, r0, :PART]
                d_im = im - projection * base[cp, r0, PART:]
                score[cp, r0] += (d_re * d_re + d_im * d_im) * tail_scale

            transforms(use_tail)
            return carry

        lax.fori_loop(0, CAL, response, 0)
        for cp in range(RADIX_C // 2):
            for r0 in range(RADIX_R):
                done = score[cp, r0] * (1.0 / (DET * RESP))
                natural[2 * cp, pl.ds(r0, PART, stride=RADIX_R)] = done[:, :PART]
                natural[2 * cp + 1, pl.ds(r0, PART, stride=RADIX_R)] = done[:, PART:]
        left = jnp.concatenate([natural[c0].astype(jnp.bfloat16) for c0 in range(RADIX_C)], axis=1)
        span = N2 // planes
        whole = jnp.dot(left, unscramble[...], preferred_element_type=jnp.float32)
        for z in range(planes):
            out[z] = whole[:, z * span : (z + 1) * span].astype(jnp.bfloat16)


def lag_scores(plan, rows, where, spectrum, tables, tmpl, psd, own, other):
    vmem = pl.BlockSpec(memory_space=pltpu.VMEM)
    hbm = pl.BlockSpec(memory_space=pl.ANY)
    streams = [*tmpl, *psd, *own, *other]
    inner_type = jnp.bfloat16 if rows % 16 == 0 else jnp.float32
    return pl.pallas_call(
        functools.partial(lag_kernel, plan, rows),
        out_shape=jax.ShapeDtypeStruct((plan.planes, N1, N2 // plan.planes), jnp.bfloat16),
        in_specs=[pl.BlockSpec(memory_space=pltpu.SMEM), *[vmem] * 5, *[hbm] * len(streams)],
        out_specs=vmem,
        scratch_shapes=[
            pltpu.VMEM((plan.freq, 2, rows, N2), jnp.bfloat16),
            pltpu.VMEM((plan.freq, rows, N2), jnp.bfloat16),
            pltpu.VMEM((CAL, plan.freq, rows, N2), jnp.bfloat16),
            pltpu.VMEM((2, N1, N2), jnp.float32),
            pltpu.VMEM((N1, N2), jnp.float32),
            pltpu.VMEM((RADIX_C, plan.freq, rows, 2 * PART), inner_type),
            pltpu.VMEM((RADIX_C // 2, RADIX_R, 2 * PART, 2 * PART), jnp.float32),
            pltpu.VMEM((RADIX_C // 2, RADIX_R, PART, 2 * PART), jnp.float32),
            pltpu.VMEM((RADIX_C, N1, PART), jnp.float32),
            pltpu.VMEM((2, 8, N2), jnp.float32),
            pltpu.SemaphoreType.DMA((3,)),
        ],
        compiler_params=pltpu.CompilerParams(vmem_limit_bytes=60 * 1024 * 1024),
        name="lag_scores",
    )(where, spectrum, *tables, *streams)


def gate(strain, gate_start, first_col):
    cols = first_col + iota(strain.shape[1])
    sample = N2 * iota(N1)[None, :] + cols[:, None]
    starts = gate_start[:, :, None, None]
    inside = (sample[None, None] >= starts) & (sample[None, None] < starts + GATE_LEN)
    return jnp.where(jnp.any(inside, axis=1), jnp.zeros_like(strain), strain)


def spectrum_of(strain):
    table_r, table_c, (tw_re, tw_im) = forward_tables()
    section = jnp.einsum("kr,cr->kc", table_r, strain, preferred_element_type=jnp.float32)
    re, im = section[:N1], section[N1:]
    out_re = re * tw_re + im * tw_im
    out_im = im * tw_re - re * tw_im
    section_one = jnp.stack([out_re, out_im]).astype(jnp.bfloat16)
    return jnp.einsum("pkc,pcq->kq", section_one, table_c, preferred_element_type=jnp.float32)


def on_device(groups, strain, gate_start, psd_inverse, templates, basis):
    freq = lax.axis_size("freq")
    plan = Plan(freq, templates.shape[0], groups)
    me = lax.axis_index("freq")
    group = lax.axis_index("tmpl")
    plane, place = me // plan.width, me % plan.width
    cols, rows = strain.shape[1], psd_inverse.shape[1]

    tmpl = scatter_templates(plan, place, templates)
    below, above = gather_templates(plan, tmpl)

    gated = gate(strain, gate_start, me * cols)
    packed = jnp.concatenate([gated[:, : cols // 2], gated[:, cols // 2 :]], axis=2)
    small = jnp.stack([packed, psd_inverse.astype(jnp.bfloat16)], axis=1)
    shared = gather_plane(plan, scatter_planes(plan, plane, small))

    mine = group % 2
    half = lax.dynamic_slice_in_dim(basis, 2 * mine, 2, 1)
    half = scatter_planes(plan, plane, half)
    other = lax.ppermute(half, "tmpl", [(g, g ^ 1) for g in range(groups)])
    own = gather_plane(plan, half)
    other = gather_plane(plan, other)

    pieces = jnp.concatenate([s[:, :, 0] for s in shared])
    pieces = pieces.reshape((freq,) + pieces.shape[2:])
    source = iota(freq)
    slots = plan.slot(place, source % plan.width) * plan.planes
    slots = slots + (plane - source // plan.width) % plan.planes
    pieces = jnp.take(pieces, slots, axis=0)
    whole = pieces.reshape(freq, cols // 2, 2, N1).transpose(0, 2, 1, 3).reshape(N2, N1)
    spectrum = spectrum_of(whole)

    where = jnp.stack([plane, place]).astype(jnp.int32)
    scores = lag_scores(
        plan, rows, where, spectrum, backward_tables(), [tmpl, *below, *above], shared, own, other
    )

    summed = pick(scores, plane).astype(jnp.float32)
    for o in range(1, plan.planes):
        got = lax.ppermute(pick(scores, (plane + o) % plan.planes), "freq", plan.shift_out(o))
        summed = summed + got.astype(jnp.float32)
    best = summed
    for b in plan.bits:
        side = (place // b) % 2
        span = best.shape[1] // 2
        send = lax.dynamic_slice_in_dim(best, (1 - side) * span, span, 1)
        keep = lax.dynamic_slice_in_dim(best, side * span, span, 1)
        best = jnp.maximum(keep, lax.ppermute(send, "freq", plan.swap(b)))
    b = groups // 2
    while b:
        side = (group // b) % 2
        span = best.shape[0] // 2
        send = lax.dynamic_slice_in_dim(best, (1 - side) * span, span, 0)
        keep = lax.dynamic_slice_in_dim(best, side * span, span, 0)
        swap = [(g, g ^ b) for g in range(groups)]
        best = jnp.maximum(keep, lax.ppermute(send, "tmpl", swap))
        b //= 2
    return best


def solution(mesh):
    placed = (
        P(None, "freq", None),
        P(),
        P(None, "freq", None),
        P("tmpl", None, "freq", None),
        P(None, None, "freq", None),
    )
    return jax.shard_map(
        functools.partial(on_device, mesh.shape["tmpl"]),
        mesh=mesh,
        in_specs=placed,
        out_specs=P("tmpl", "freq"),
        check_vma=False,
    )
```

```python
import functools
import math

import jax
import jax.numpy as jnp
from jax import lax
from jax.experimental import pallas as pl
from jax.experimental.pallas import tpu as pltpu
from jax.sharding import PartitionSpec as P


N1 = 512
N2 = 1024
DET = 3
CAL = 4
RESP = 5
GATE_LEN = 4096
MODULUS = N1 * N2
RADIX_C = 8
RADIX_R = 4
PART = 128
HALF_ROOT = math.sqrt(0.5)


def phase(products, length):
    angles = (products % length).astype(jnp.float32) * (2.0 * math.pi / length)
    return jnp.cos(angles), jnp.sin(angles)


def times(left, right):
    return left[0] * right[0] - left[1] * right[1], left[0] * right[1] + left[1] * right[0]


def product_phase(rows, cols, length):
    fine = jnp.arange(32, dtype=jnp.int32)
    coarse = 32 * jnp.arange(rows // 32, dtype=jnp.int32)
    high = phase(coarse[:, None] * cols, length)
    low = phase(fine[:, None] * cols, length)
    real, imag = times([h[:, None] for h in high], [w[None] for w in low])
    return real.reshape(rows, -1), imag.reshape(rows, -1)


def iota(count):
    return jnp.arange(count, dtype=jnp.int32)


def row_table(zero):
    cos_r, sin_r = product_phase(N1, zero + iota(N1)[None], N1)
    return jnp.concatenate([cos_r, -sin_r], axis=0).astype(jnp.bfloat16)


def block_table(real, imag, transposed):
    up, low = (-imag, imag) if transposed else (imag, -imag)
    top = jnp.concatenate([real, up], axis=2)
    return jnp.concatenate([top, jnp.concatenate([low, real], axis=2)], axis=1).astype(jnp.bfloat16)


def lag_columns(zero):
    return zero + iota(RADIX_C)[:, None] + RADIX_C * iota(PART)[None, :]


def column_tables(zero):
    cols = lag_columns(zero)
    stage_one = block_table(*phase(iota(PART)[None, :, None] * cols[:, None, :], N2), False)
    coarse = 32 * iota(N1 // 32)
    high = phase(coarse[None, :, None] * cols[:, None, :], MODULUS)
    low = phase(iota(32)[None, :, None] * cols[:, None, :], MODULUS)
    real, imag = times([h[:, :, None] for h in high], [w[:, None] for w in low])
    twiddle = jnp.concatenate([real, imag], axis=3).reshape(RADIX_C, N1, 2 * PART)
    return stage_one, twiddle


def lag_tables(zero):
    rows = zero + iota(RADIX_R)[:, None] + RADIX_R * iota(PART)[None, :]
    stage_two = block_table(*phase(rows[:, :, None] * iota(PART)[None, None, :], N1), True)
    order = lag_columns(zero).reshape(-1)
    unscramble = (order[:, None] == iota(N2)[None, :]).astype(jnp.bfloat16)
    return stage_two, unscramble


class Plan:
    def __init__(self, freq, templates, groups):
        self.freq, self.width, self.groups = freq, templates, groups
        self.planes = freq // templates
        self.bits = [1 << b for b in reversed(range(templates.bit_length() - 1))]
        self.offsets = [0]
        for b in self.bits:
            self.offsets = self.offsets + [o ^ b for o in self.offsets]

    def swap(self, bit):
        return [(f, f ^ bit) for f in range(self.freq)]

    def devices(self, pairs):
        w = self.width
        return [(a * w + k, b * w + k) for a, b in pairs for k in range(w)]

    def shift_in(self, o):
        n = self.planes
        return self.devices([(z, (z + o) % n) for z in range(n) if (z + o) % n < DET])

    def shift_out(self, o):
        n = self.planes
        return self.devices([(z, (z + o) % n) for z in range(DET)])

    def back(self):
        n = self.planes
        return self.devices([(z, (z - 1) % n) for z in range(n)])


def pick(array, index, axis=0):
    return lax.dynamic_index_in_dim(array, index, axis, keepdims=False)


def scatter_planes(plan, plane, array):
    got = [pick(array, jnp.minimum(plane, DET - 1))]
    for o in range(1, plan.planes):
        send = pick(array, jnp.minimum((plane + o) % plan.planes, DET - 1))
        got.append(lax.ppermute(send, "freq", plan.shift_in(o)))
    return jnp.stack(got)


def gather_plane(plan, piece):
    held = piece[None]
    pieces = [held]
    for b in plan.bits:
        got = lax.ppermute(held, "freq", plan.swap(b))
        pieces.append(got)
        held = jnp.concatenate([held, got])
    return pieces


def scatter_templates(plan, place, templates):
    held = templates[None]
    for b in plan.bits:
        mine = (place // b) % 2
        halves = held.reshape((held.shape[0], 2, held.shape[1] // 2) + held.shape[2:])
        got = lax.ppermute(pick(halves, 1 - mine, 1), "freq", plan.swap(b))
        held = jnp.concatenate([pick(halves, mine, 1), got])
    return held[:, 0]


def gather_templates(plan, piece):
    pieces = [piece]
    for _ in range(1, plan.planes):
        pieces.append(lax.ppermute(pieces[-1], "freq", plan.back()))
    return pieces


def dft_eight(real, imag):
    def add(a, b):
        return real_imag[a][0] + real_imag[b][0], real_imag[a][1] + real_imag[b][1]

    def sub(a, b):
        return real_imag[a][0] - real_imag[b][0], real_imag[a][1] - real_imag[b][1]

    real_imag = list(zip(real, imag))
    a0, a1 = add(0, 4), sub(0, 4)
    a2, a3 = add(2, 6), sub(2, 6)
    a4, a5 = add(1, 5), sub(1, 5)
    a6, a7 = add(3, 7), sub(3, 7)
    e0 = (a0[0] + a2[0], a0[1] + a2[1])
    e1 = (a0[0] - a2[0], a0[1] - a2[1])
    o0 = (a4[0] + a6[0], a4[1] + a6[1])
    o1 = (a4[0] - a6[0], a4[1] - a6[1])
    f0 = (a1[0] - a3[1], a1[1] + a3[0])
    f1 = (a1[0] + a3[1], a1[1] - a3[0])
    m = (HALF_ROOT * (a5[0] - a7[0]), HALF_ROOT * (a5[1] - a7[1]))
    n = (HALF_ROOT * (a5[0] + a7[0]), HALF_ROOT * (a5[1] + a7[1]))
    g0 = (m[0] - n[1], m[1] + n[0])
    g1 = (-m[0] - n[1], n[0] - m[1])
    return [
        (e0[0] + o0[0], e0[1] + o0[1]),
        (f0[0] + g0[0], f0[1] + g0[1]),
        (e1[0] - o1[1], e1[1] + o1[0]),
        (f1[0] + g1[0], f1[1] + g1[1]),
        (e0[0] - o0[0], e0[1] - o0[1]),
        (f0[0] - g0[0], f0[1] - g0[1]),
        (e1[0] + o1[1], e1[1] - o1[0]),
        (f1[0] - g1[0], f1[1] - g1[1]),
    ]


def dft_four(real, imag):
    s0, s1 = (real[0] + real[2], imag[0] + imag[2]), (real[0] - real[2], imag[0] - imag[2])
    t0, t1 = (real[1] + real[3], imag[1] + imag[3]), (real[1] - real[3], imag[1] - imag[3])
    return [
        (s0[0] + t0[0], s0[1] + t0[1]),
        (s1[0] - t1[1], s1[1] + t1[0]),
        (s0[0] - t0[0], s0[1] - t0[1]),
        (s1[0] + t1[1], s1[1] - t1[0]),
    ]


def from_plane_gather(plan, plane, place, pieces, put):
    m = 0
    for piece in pieces:
        for i in range(piece.shape[0]):
            for o in range(plan.planes):
                behind = lax.rem(plane - o + plan.planes, plan.planes)
                put(piece.at[i, o], behind * plan.width + (place ^ plan.offsets[m]))
            m += 1


def spectrum_kernel(plan, rows, where_ref, gates_ref, row_table_ref, stage_one, twiddle, *rest):
    pieces, rest = rest[: 1 + len(plan.bits)], rest[1 + len(plan.bits) :]
    out, blocks, samples, parts, sem = rest
    plane, place = where_ref[0], where_ref[1]

    @pl.when(plane < DET)
    def _():
        from_plane_gather(
            plan,
            plane,
            place,
            pieces,
            lambda src, f: pltpu.make_async_copy(src, blocks.at[f], sem).start(),
        )
        pltpu.make_async_copy(blocks, blocks, sem).wait()
        tiles = N1 // PART

        starts = [gates_ref[plane, g] for g in range(gates_ref.shape[1])]
        step = lax.broadcasted_iota(jnp.int32, (rows, PART), 0)
        step = step + N2 * lax.broadcasted_iota(jnp.int32, (rows, PART), 1)

        def spread(block, carry):
            piece = blocks[block, 0].astype(jnp.float32)
            for half in range(2):
                at = pl.ds(pl.multiple_of((2 * block + half) * rows, rows), rows)
                for t in range(tiles):
                    first = half * N1 + t * PART
                    values = piece[:, first : first + PART]
                    for start in starts:
                        past = step + ((2 * block + half) * rows + t * PART * N2 - start)
                        values = jnp.where((past >= 0) & (past < GATE_LEN), 0.0, values)
                    samples[t, at] = values
            return carry

        lax.fori_loop(0, plan.freq, spread, 0)
        for a in range(RADIX_C):
            right = [samples[t, pl.ds(a, PART, stride=RADIX_C)] for t in range(tiles)]
            right = jnp.concatenate([r.astype(jnp.bfloat16) for r in right], axis=1)
            section = lax.dot_general(
                row_table_ref[...],
                right,
                (((1,), (1,)), ((), ())),
                preferred_element_type=jnp.float32,
            )
            re, im = section[:N1], section[N1:]
            tw_re, tw_im = twiddle[a, :, :PART], twiddle[a, :, PART:]
            both = [re * tw_re + im * tw_im, im * tw_re - re * tw_im]
            both = jnp.concatenate(both, axis=1).astype(jnp.bfloat16)
            parts[a] = lax.dot_general(
                both, stage_one[a], (((1,), (1,)), ((), ())), preferred_element_type=jnp.float32
            )

        def finish(block, carry):
            at = pl.ds(pl.multiple_of(block * rows, rows), rows)
            inverse = blocks[block, 1].astype(jnp.float32)
            re = [parts[a, at, :PART] for a in range(RADIX_C)]
            im = [parts[a, at, PART:] for a in range(RADIX_C)]
            for q, (y_im, y_re) in enumerate(dft_eight(im, re)):
                tile = slice(q * PART, (q + 1) * PART)
                out[0, at, tile] = y_re * inverse[:, tile]
                out[1, at, tile] = y_im * inverse[:, tile]
            return carry

        lax.fori_loop(0, plan.freq, finish, 0)


def spectrum_of(plan, rows, where, gates, table_r, stage_one, twiddle, pieces):
    vmem = pl.BlockSpec(memory_space=pltpu.VMEM)
    hbm = pl.BlockSpec(memory_space=pl.ANY)
    return pl.pallas_call(
        functools.partial(spectrum_kernel, plan, rows),
        out_shape=jax.ShapeDtypeStruct((2, N1, N2), jnp.float32),
        in_specs=[*[pl.BlockSpec(memory_space=pltpu.SMEM)] * 2, *[vmem] * 3, *[hbm] * len(pieces)],
        out_specs=vmem,
        scratch_shapes=[
            pltpu.VMEM((plan.freq, 2, rows, N2), jnp.bfloat16),
            pltpu.VMEM((N1 // PART, N2, PART), jnp.float32),
            pltpu.VMEM((RADIX_C, N1, 2 * PART), jnp.float32),
            pltpu.SemaphoreType.DMA,
        ],
        compiler_params=pltpu.CompilerParams(vmem_limit_bytes=40 * 1024 * 1024),
        name="spectrum",
    )(where, gates, table_r, stage_one, twiddle, *pieces)


def total(array):
    return jnp.sum(jnp.sum(array, axis=0, keepdims=True), axis=1, keepdims=True)


def lag_kernel(
    plan, rows, where_ref, spectrum, stage_one, stage_two, twiddle, unscramble, *rest
):
    n_tmpl = plan.planes
    n_piece = 1 + len(plan.bits)
    tmpl_in, rest = rest[:n_tmpl], rest[n_tmpl:]
    small_in, rest = rest[:n_piece], rest[n_piece:]
    own_in, rest = rest[:n_piece], rest[n_piece:]
    other_in, rest = rest[:n_piece], rest[n_piece:]
    outs, rest = rest[: plan.planes], rest[plan.planes :]
    tmpl, psd, basis, prod, weight, inner, score, natural, blocks, acc, sem = rest
    plane, place = where_ref[0], where_ref[1]
    freq, width, planes = plan.freq, plan.width, plan.planes

    @pl.when(plane >= DET)
    def _():
        for ref in outs:
            ref[...] = jnp.zeros_like(ref)

    @pl.when(plane < DET)
    def _():
        def copy_tmpl(ref, source_plane):
            for m in range(width):
                source = source_plane * width + (place ^ plan.offsets[m])
                pltpu.make_async_copy(ref.at[m], tmpl.at[source], sem.at[0]).start()

        for ahead, ref in enumerate(tmpl_in):
            copy_tmpl(ref, lax.rem(plane + ahead, planes))

        from_pieces = functools.partial(from_plane_gather, plan, plane, place)
        from_pieces(
            small_in, lambda src, f: pltpu.make_async_copy(src.at[1], psd.at[f], sem.at[1]).start()
        )
        for j in range(2):
            from_pieces(
                own_in,
                lambda src, f, j=j: pltpu.make_async_copy(
                    src.at[j], basis.at[j, f], sem.at[2]
                ).start(),
            )
            from_pieces(
                other_in,
                lambda src, f, j=j: pltpu.make_async_copy(
                    src.at[j], basis.at[2 + j, f], sem.at[2]
                ).start(),
            )
        pltpu.make_async_copy(tmpl, tmpl, sem.at[0]).wait()
        pltpu.make_async_copy(psd, psd, sem.at[1]).wait()

        def spread_out(block, real, imag):
            tiles = [slice(a * PART, (a + 1) * PART) for a in range(RADIX_C)]
            parts = dft_eight([real[:, t] for t in tiles], [imag[:, t] for t in tiles])
            for c0, (re, im) in enumerate(parts):
                both = jnp.concatenate([re, im], axis=1)
                inner[c0, block] = both.astype(inner.dtype)

        def fold(array):
            return jnp.sum(array.reshape(rows // 8, 8, N2), axis=0)

        acc[...] = jnp.zeros_like(acc)

        def start_block(block, carry):
            at = pl.ds(pl.multiple_of(block * rows, rows), rows)
            t_re = tmpl[block, 0].astype(jnp.float32)
            t_im = tmpl[block, 1].astype(jnp.float32)
            inverse = psd[block].astype(jnp.float32)
            x_re = spectrum[0, at]
            x_im = spectrum[1, at]
            p_re = x_re * t_re + x_im * t_im
            p_im = x_im * t_re - x_re * t_im
            heavy = inverse * inverse * (t_re * t_re + t_im * t_im)
            prod[0, at] = p_re
            prod[1, at] = p_im
            weight[at] = heavy
            acc[0] += fold(heavy)
            spread_out(block, p_re, p_im)
            return carry

        lax.fori_loop(0, freq, start_block, 0)
        variance = total(acc[0])

        def transforms(use):
            def pair(cp, carry):
                columns = [[] for _ in range(RADIX_R)]
                for half in range(2):
                    c0 = 2 * cp + half
                    left = inner[c0].reshape(N1, 2 * PART).astype(jnp.bfloat16)
                    lag = jnp.dot(left, stage_one[c0], preferred_element_type=jnp.float32)
                    g_re, g_im = lag[:, :PART], lag[:, PART:]
                    tw_re, tw_im = twiddle[c0, :, :PART], twiddle[c0, :, PART:]
                    y_re = g_re * tw_re - g_im * tw_im
                    y_im = g_re * tw_im + g_im * tw_re
                    cuts = [slice(a * PART, (a + 1) * PART) for a in range(RADIX_R)]
                    parts = dft_four([y_re[t] for t in cuts], [y_im[t] for t in cuts])
                    for r0, (re, im) in enumerate(parts):
                        columns[r0].append(jnp.concatenate([re, im], axis=0).astype(jnp.bfloat16))
                for r0 in range(RADIX_R):
                    right = jnp.concatenate(columns[r0], axis=1)
                    lag = jnp.dot(stage_two[r0], right, preferred_element_type=jnp.float32)
                    use(cp, r0, lag[:PART], lag[PART:])
                return carry

            lax.fori_loop(0, RADIX_C // 2, pair, 0)

        head_scale = 1.0 / (MODULUS * variance)

        def use_base(cp, r0, re, im):
            score[cp, r0] = (re * re + im * im) * head_scale

        transforms(use_base)
        pltpu.make_async_copy(basis, basis, sem.at[2]).wait()

        acc[...] = jnp.zeros_like(acc)

        def moment_block(block, carry):
            at = pl.ds(pl.multiple_of(block * rows, rows), rows)
            heavy = weight[at]
            for j in range(CAL):
                acc[j] += fold(heavy * basis[j, block].astype(jnp.float32))
            return carry

        lax.fori_loop(0, freq, moment_block, 0)

        def response(j, carry):
            projection = total(acc[j]) / variance
            acc[CAL] = jnp.zeros_like(acc[CAL])

            def filter_block(block, inside):
                at = pl.ds(pl.multiple_of(block * rows, rows), rows)
                centred = basis[j, block].astype(jnp.float32) - projection
                acc[CAL] += fold(weight[at] * centred * centred)
                spread_out(block, prod[0, at] * centred, prod[1, at] * centred)
                return inside

            lax.fori_loop(0, freq, filter_block, 0)
            tail_scale = 1.0 / (MODULUS * total(acc[CAL]))

            def use_tail(cp, r0, re, im):
                score[cp, r0] += (re * re + im * im) * tail_scale

            transforms(use_tail)
            return carry

        lax.fori_loop(0, CAL, response, 0)
        for cp in range(RADIX_C // 2):
            for r0 in range(RADIX_R):
                done = score[cp, r0] * (1.0 / (DET * RESP))
                natural[2 * cp, pl.ds(r0, PART, stride=RADIX_R)] = done[:, :PART]
                natural[2 * cp + 1, pl.ds(r0, PART, stride=RADIX_R)] = done[:, PART:]
        left = jnp.concatenate([natural[c0].astype(jnp.bfloat16) for c0 in range(RADIX_C)], axis=1)
        span = N2 // planes
        whole = jnp.dot(left, unscramble[...], preferred_element_type=jnp.float32)
        for z in range(planes):
            blocks[z] = whole[:, z * span : (z + 1) * span]
        for o, ref in enumerate(outs):
            ref[...] = blocks[lax.rem(plane + o, planes)].astype(jnp.bfloat16)


def lag_scores(plan, rows, where, spectrum, tables, tmpl, small, own, other):
    vmem = pl.BlockSpec(memory_space=pltpu.VMEM)
    hbm = pl.BlockSpec(memory_space=pl.ANY)
    streams = [*tmpl, *small, *own, *other]
    inner_type = jnp.bfloat16 if rows % 16 == 0 else jnp.float32
    return pl.pallas_call(
        functools.partial(lag_kernel, plan, rows),
        out_shape=[jax.ShapeDtypeStruct((N1, N2 // plan.planes), jnp.bfloat16)] * plan.planes,
        in_specs=[pl.BlockSpec(memory_space=pltpu.SMEM), *[vmem] * 5, *[hbm] * len(streams)],
        out_specs=[vmem] * plan.planes,
        scratch_shapes=[
            pltpu.VMEM((plan.freq, 2, rows, N2), jnp.bfloat16),
            pltpu.VMEM((plan.freq, rows, N2), jnp.bfloat16),
            pltpu.VMEM((CAL, plan.freq, rows, N2), jnp.bfloat16),
            pltpu.VMEM((2, N1, N2), jnp.float32),
            pltpu.VMEM((N1, N2), jnp.float32),
            pltpu.VMEM((RADIX_C, plan.freq, rows, 2 * PART), inner_type),
            pltpu.VMEM((RADIX_C // 2, RADIX_R, PART, 2 * PART), jnp.float32),
            pltpu.VMEM((RADIX_C, N1, PART), jnp.float32),
            pltpu.VMEM((plan.planes, N1, N2 // plan.planes), jnp.float32),
            pltpu.VMEM((CAL + 1, 8, N2), jnp.float32),
            pltpu.SemaphoreType.DMA((3,)),
        ],
        compiler_params=pltpu.CompilerParams(vmem_limit_bytes=60 * 1024 * 1024),
        name="lag_scores",
    )(where, spectrum, *tables, *streams)


def on_device(groups, strain, gate_start, psd_inverse, templates, basis):
    freq = lax.axis_size("freq")
    plan = Plan(freq, templates.shape[0], groups)
    me = lax.axis_index("freq")
    group = lax.axis_index("tmpl")
    plane, place = me // plan.width, me % plan.width
    cols, rows = strain.shape[1], psd_inverse.shape[1]

    packed = jnp.concatenate([strain[:, : cols // 2], strain[:, cols // 2 :]], axis=2)
    half = lax.dynamic_slice_in_dim(basis, 2 * (group % 2), 2, 1)
    inverse = psd_inverse.astype(jnp.bfloat16)
    shares = jnp.concatenate([packed[:, None], inverse[:, None], half], axis=1)
    piece = scatter_planes(plan, plane, shares)

    tmpl = scatter_templates(plan, place, templates)
    rings = gather_templates(plan, tmpl)

    small = gather_plane(plan, piece[:, :2])
    other = lax.ppermute(piece[:, 2:], "tmpl", [(g, g ^ 1) for g in range(groups)])
    own = gather_plane(plan, piece[:, 2:])
    other = gather_plane(plan, other)

    where = jnp.stack([plane, place]).astype(jnp.int32)
    zero, _ = lax.optimization_barrier((jnp.int32(0), tmpl))
    stage_one, twiddle = column_tables(zero)
    table_r = row_table(zero)
    stage_two, unscramble = lag_tables(zero)
    spectrum = spectrum_of(plan, rows, where, gate_start, table_r, stage_one, twiddle, small)
    scores = lag_scores(
        plan,
        rows,
        where,
        spectrum,
        (stage_one, stage_two, twiddle, unscramble),
        rings,
        small,
        own,
        other,
    )

    summed = scores[0].astype(jnp.float32)
    for o in range(1, plan.planes):
        got = lax.ppermute(scores[o], "freq", plan.shift_out(o))
        summed = summed + got.astype(jnp.float32)
    best = summed.astype(jnp.bfloat16)
    for b in plan.bits:
        side = (place // b) % 2
        span = best.shape[1] // 2
        send = lax.dynamic_slice_in_dim(best, (1 - side) * span, span, 1)
        keep = lax.dynamic_slice_in_dim(best, side * span, span, 1)
        best = jnp.maximum(keep, lax.ppermute(send, "freq", plan.swap(b)))
    b = groups // 2
    while b:
        side = (group // b) % 2
        span = best.shape[0] // 2
        send = lax.dynamic_slice_in_dim(best, (1 - side) * span, span, 0)
        keep = lax.dynamic_slice_in_dim(best, side * span, span, 0)
        swap = [(g, g ^ b) for g in range(groups)]
        best = jnp.maximum(keep, lax.ppermute(send, "tmpl", swap))
        b //= 2
    return best.astype(jnp.float32)


def solution(mesh):
    def whole(*args):
        return on_device(mesh.shape["tmpl"], *args)

    placed = (
        P(None, "freq", None),
        P(),
        P(None, "freq", None),
        P("tmpl", None, "freq", None),
        P(None, None, "freq", None),
    )
    return jax.shard_map(
        whole, mesh=mesh, in_specs=placed, out_specs=P("tmpl", "freq"), check_vma=False
    )
```

```python
import functools
import math

import jax
import jax.numpy as jnp
from jax import lax
from jax.experimental import pallas as pl
from jax.experimental.pallas import tpu as pltpu
from jax.sharding import PartitionSpec as P


N1 = 512
N2 = 1024
DET = 3
CAL = 4
RESP = 5
GATE_LEN = 4096
MODULUS = N1 * N2
RADIX_C = 8
RADIX_R = 4
PART = 128
HALF_ROOT = math.sqrt(0.5)


def phase(products, length):
    angles = (products % length).astype(jnp.float32) * (2.0 * math.pi / length)
    return jnp.cos(angles), jnp.sin(angles)


def times(left, right):
    return left[0] * right[0] - left[1] * right[1], left[0] * right[1] + left[1] * right[0]


def product_phase(rows, cols, length):
    fine = jnp.arange(32, dtype=jnp.int32)
    coarse = 32 * jnp.arange(rows // 32, dtype=jnp.int32)
    high = phase(coarse[:, None] * cols, length)
    low = phase(fine[:, None] * cols, length)
    real, imag = times([h[:, None] for h in high], [w[None] for w in low])
    return real.reshape(rows, -1), imag.reshape(rows, -1)


def iota(count):
    return jnp.arange(count, dtype=jnp.int32)


def row_table(zero):
    cos_r, sin_r = product_phase(N1, zero + iota(N1)[None], N1)
    return jnp.concatenate([cos_r, -sin_r], axis=0).astype(jnp.bfloat16)


def block_table(real, imag, transposed):
    up, low = (-imag, imag) if transposed else (imag, -imag)
    top = jnp.concatenate([real, up], axis=2)
    return jnp.concatenate([top, jnp.concatenate([low, real], axis=2)], axis=1).astype(jnp.bfloat16)


def lag_columns(zero):
    return zero + iota(RADIX_C)[:, None] + RADIX_C * iota(PART)[None, :]


def column_tables(zero):
    cols = lag_columns(zero)
    stage_one = block_table(*phase(iota(PART)[None, :, None] * cols[:, None, :], N2), False)
    coarse = 32 * iota(N1 // 32)
    high = phase(coarse[None, :, None] * cols[:, None, :], MODULUS)
    low = phase(iota(32)[None, :, None] * cols[:, None, :], MODULUS)
    return stage_one, jnp.stack(high), jnp.stack(low)


def lag_tables(zero):
    rows = zero + iota(RADIX_R)[:, None] + RADIX_R * iota(PART)[None, :]
    stage_two = block_table(*phase(rows[:, :, None] * iota(PART)[None, None, :], N1), True)
    return stage_two


class Plan:
    def __init__(self, freq, templates, groups):
        self.freq, self.width, self.groups = freq, templates, groups
        self.planes = freq // templates
        self.bits = [1 << b for b in reversed(range(templates.bit_length() - 1))]
        self.offsets = [0]
        for b in self.bits:
            self.offsets = self.offsets + [o ^ b for o in self.offsets]

    def swap(self, bit):
        return [(f, f ^ bit) for f in range(self.freq)]

    def devices(self, pairs):
        w = self.width
        return [(a * w + k, b * w + k) for a, b in pairs for k in range(w)]

    def shift_in(self, o):
        n = self.planes
        return self.devices([(z, (z + o) % n) for z in range(n) if (z + o) % n < DET])

    def shift_out(self, o):
        n = self.planes
        return self.devices([(z, (z + o) % n) for z in range(DET)])

    def back(self):
        n = self.planes
        return self.devices([(z, (z - 1) % n) for z in range(n)])


def pick(array, index, axis=0):
    return lax.dynamic_index_in_dim(array, index, axis, keepdims=False)


def scatter_planes(plan, plane, array):
    got = [pick(array, jnp.minimum(plane, DET - 1))]
    for o in range(1, plan.planes):
        send = pick(array, jnp.minimum((plane + o) % plan.planes, DET - 1))
        got.append(lax.ppermute(send, "freq", plan.shift_in(o)))
    return jnp.stack(got)


def gather_plane(plan, piece):
    held = piece[None]
    pieces = [held]
    for b in plan.bits:
        got = lax.ppermute(held, "freq", plan.swap(b))
        pieces.append(got)
        held = jnp.concatenate([held, got])
    return pieces


def scatter_templates(plan, place, templates):
    held = templates[None]
    for b in plan.bits:
        mine = (place // b) % 2
        halves = held.reshape((held.shape[0], 2, held.shape[1] // 2) + held.shape[2:])
        got = lax.ppermute(pick(halves, 1 - mine, 1), "freq", plan.swap(b))
        held = jnp.concatenate([pick(halves, mine, 1), got])
    return held[:, 0]


def gather_templates(plan, piece):
    pieces = [piece]
    for _ in range(1, plan.planes):
        pieces.append(lax.ppermute(pieces[-1], "freq", plan.back()))
    return pieces


def dft_eight(real, imag):
    def add(a, b):
        return real_imag[a][0] + real_imag[b][0], real_imag[a][1] + real_imag[b][1]

    def sub(a, b):
        return real_imag[a][0] - real_imag[b][0], real_imag[a][1] - real_imag[b][1]

    real_imag = list(zip(real, imag))
    a0, a1 = add(0, 4), sub(0, 4)
    a2, a3 = add(2, 6), sub(2, 6)
    a4, a5 = add(1, 5), sub(1, 5)
    a6, a7 = add(3, 7), sub(3, 7)
    e0 = (a0[0] + a2[0], a0[1] + a2[1])
    e1 = (a0[0] - a2[0], a0[1] - a2[1])
    o0 = (a4[0] + a6[0], a4[1] + a6[1])
    o1 = (a4[0] - a6[0], a4[1] - a6[1])
    f0 = (a1[0] - a3[1], a1[1] + a3[0])
    f1 = (a1[0] + a3[1], a1[1] - a3[0])
    m = (HALF_ROOT * (a5[0] - a7[0]), HALF_ROOT * (a5[1] - a7[1]))
    n = (HALF_ROOT * (a5[0] + a7[0]), HALF_ROOT * (a5[1] + a7[1]))
    g0 = (m[0] - n[1], m[1] + n[0])
    g1 = (-m[0] - n[1], n[0] - m[1])
    return [
        (e0[0] + o0[0], e0[1] + o0[1]),
        (f0[0] + g0[0], f0[1] + g0[1]),
        (e1[0] - o1[1], e1[1] + o1[0]),
        (f1[0] + g1[0], f1[1] + g1[1]),
        (e0[0] - o0[0], e0[1] - o0[1]),
        (f0[0] - g0[0], f0[1] - g0[1]),
        (e1[0] + o1[1], e1[1] - o1[0]),
        (f1[0] - g1[0], f1[1] - g1[1]),
    ]


def dft_four(real, imag):
    s0, s1 = (real[0] + real[2], imag[0] + imag[2]), (real[0] - real[2], imag[0] - imag[2])
    t0, t1 = (real[1] + real[3], imag[1] + imag[3]), (real[1] - real[3], imag[1] - imag[3])
    return [
        (s0[0] + t0[0], s0[1] + t0[1]),
        (s1[0] - t1[1], s1[1] + t1[0]),
        (s0[0] - t0[0], s0[1] - t0[1]),
        (s1[0] + t1[1], s1[1] - t1[0]),
    ]


def from_plane_gather(plan, plane, place, pieces, put):
    m = 0
    for piece in pieces:
        for i in range(piece.shape[0]):
            for o in range(plan.planes):
                behind = lax.rem(plane - o + plan.planes, plan.planes)
                put(piece.at[i, o], behind * plan.width + (place ^ plan.offsets[m]))
            m += 1


def spectrum_kernel(
    plan, rows, where_ref, gates_ref, row_table_ref, stage_one, coarse_ref, fine_ref, *rest
):
    pieces, rest = rest[: 1 + len(plan.bits)], rest[1 + len(plan.bits) :]
    out, twiddle, unscramble, blocks, samples, parts, sem = rest
    plane, place = where_ref[0], where_ref[1]

    @pl.when(plane < DET)
    def _():
        from_plane_gather(
            plan,
            plane,
            place,
            pieces,
            lambda src, f: pltpu.make_async_copy(src, blocks.at[f], sem).start(),
        )

        def twiddle_of(c0, carry):
            fine_re, fine_im = fine_ref[0, c0], fine_ref[1, c0]
            span = fine_re.shape[0]
            for a in range(N1 // span):
                high = coarse_ref[0, c0, a : a + 1], coarse_ref[1, c0, a : a + 1]
                re, im = times(high, (fine_re, fine_im))
                twiddle[c0, a * span : (a + 1) * span, :PART] = re
                twiddle[c0, a * span : (a + 1) * span, PART:] = im
            return carry

        lax.fori_loop(0, RADIX_C, twiddle_of, 0)
        row = lax.broadcasted_iota(jnp.int32, (PART, N2), 0)
        column = lax.broadcasted_iota(jnp.int32, (PART, N2), 1)
        for c0 in range(RADIX_C):
            hit = column == c0 + RADIX_C * row
            unscramble[c0 * PART : (c0 + 1) * PART] = jnp.where(hit, 1.0, 0.0).astype(jnp.bfloat16)
        pltpu.make_async_copy(blocks, blocks, sem).wait()
        tiles = N1 // PART

        starts = [gates_ref[plane, g] for g in range(gates_ref.shape[1])]
        step = lax.broadcasted_iota(jnp.int32, (rows, PART), 0)
        step = step + N2 * lax.broadcasted_iota(jnp.int32, (rows, PART), 1)

        def spread(block, carry):
            piece = blocks[block, 0].astype(jnp.float32)
            for half in range(2):
                at = pl.ds(pl.multiple_of((2 * block + half) * rows, rows), rows)
                for t in range(tiles):
                    first = half * N1 + t * PART
                    values = piece[:, first : first + PART]
                    for start in starts:
                        past = step + ((2 * block + half) * rows + t * PART * N2 - start)
                        values = jnp.where((past >= 0) & (past < GATE_LEN), 0.0, values)
                    samples[t, at] = values
            return carry

        lax.fori_loop(0, plan.freq, spread, 0)
        for first in range(0, RADIX_C, 2):
            right = []
            for a in (first, first + 1):
                found = [samples[t, pl.ds(a, PART, stride=RADIX_C)] for t in range(tiles)]
                right.append(jnp.concatenate([r.astype(jnp.bfloat16) for r in found], axis=1))
            section = lax.dot_general(
                row_table_ref[...],
                jnp.concatenate(right, axis=0),
                (((1,), (1,)), ((), ())),
                preferred_element_type=jnp.float32,
            )
            for a in (first, first + 1):
                lanes = slice((a - first) * PART, (a - first + 1) * PART)
                re, im = section[:N1, lanes], section[N1:, lanes]
                tw_re, tw_im = twiddle[a, :, :PART], twiddle[a, :, PART:]
                both = [re * tw_re + im * tw_im, im * tw_re - re * tw_im]
                both = jnp.concatenate(both, axis=1).astype(jnp.bfloat16)
                parts[a] = lax.dot_general(
                    both, stage_one[a], (((1,), (1,)), ((), ())), preferred_element_type=jnp.float32
                )

        def finish(block, carry):
            at = pl.ds(pl.multiple_of(block * rows, rows), rows)
            inverse = blocks[block, 1].astype(jnp.float32)
            re = [parts[a, at, :PART] for a in range(RADIX_C)]
            im = [parts[a, at, PART:] for a in range(RADIX_C)]
            for q, (y_im, y_re) in enumerate(dft_eight(im, re)):
                tile = slice(q * PART, (q + 1) * PART)
                out[0, at, tile] = y_re * inverse[:, tile]
                out[1, at, tile] = y_im * inverse[:, tile]
            return carry

        lax.fori_loop(0, plan.freq, finish, 0)


def spectrum_of(plan, rows, where, gates, table_r, stage_one, coarse, fine, pieces):
    vmem = pl.BlockSpec(memory_space=pltpu.VMEM)
    hbm = pl.BlockSpec(memory_space=pl.ANY)
    return pl.pallas_call(
        functools.partial(spectrum_kernel, plan, rows),
        out_shape=[
            jax.ShapeDtypeStruct((2, N1, N2), jnp.float32),
            jax.ShapeDtypeStruct((RADIX_C, N1, 2 * PART), jnp.float32),
            jax.ShapeDtypeStruct((N2, N2), jnp.bfloat16),
        ],
        in_specs=[*[pl.BlockSpec(memory_space=pltpu.SMEM)] * 2, *[vmem] * 4, *[hbm] * len(pieces)],
        out_specs=[vmem] * 3,
        scratch_shapes=[
            pltpu.VMEM((plan.freq, 2, rows, N2), jnp.bfloat16),
            pltpu.VMEM((N1 // PART, N2, PART), jnp.float32),
            pltpu.VMEM((RADIX_C, N1, 2 * PART), jnp.float32),
            pltpu.SemaphoreType.DMA,
        ],
        compiler_params=pltpu.CompilerParams(vmem_limit_bytes=40 * 1024 * 1024),
        name="spectrum",
    )(where, gates, table_r, stage_one, coarse, fine, *pieces)


def total(array):
    return jnp.sum(jnp.sum(array, axis=0, keepdims=True), axis=1, keepdims=True)


def lag_kernel(
    plan, rows, where_ref, spectrum, stage_one, stage_two, twiddle, unscramble, *rest
):
    n_tmpl = plan.planes
    n_piece = 1 + len(plan.bits)
    tmpl_in, rest = rest[:n_tmpl], rest[n_tmpl:]
    small_in, rest = rest[:n_piece], rest[n_piece:]
    own_in, rest = rest[:n_piece], rest[n_piece:]
    other_in, rest = rest[:n_piece], rest[n_piece:]
    outs, rest = rest[: plan.planes], rest[plan.planes :]
    tmpl, psd, basis, prod, weight, inner, score, natural, blocks, acc = rest
    plane, place = where_ref[0], where_ref[1]
    freq, width, planes = plan.freq, plan.width, plan.planes

    @pl.when(plane >= DET)
    def _():
        for ref in outs:
            ref[...] = jnp.zeros_like(ref)

    @pl.when(plane < DET)
    def _():
        for ahead, ref in enumerate(tmpl_in):
            source = lax.rem(plane + ahead, planes) * width
            for m in range(width):
                tmpl[source + (place ^ plan.offsets[m])] = ref[m]

        def put(target, select):
            def store(piece, f):
                target[f] = select(piece)

            return store

        from_pieces = functools.partial(from_plane_gather, plan, plane, place)
        from_pieces(small_in, put(psd, lambda p: p[1]))
        for j in range(2):
            from_pieces(own_in, put(basis.at[j], lambda p, j=j: p[j]))
            from_pieces(other_in, put(basis.at[2 + j], lambda p, j=j: p[j]))

        chunks = PART // rows

        def spread_out(block, real, imag):
            tiles = [slice(a * PART, (a + 1) * PART) for a in range(RADIX_C)]
            parts = dft_eight([real[:, t] for t in tiles], [imag[:, t] for t in tiles])
            place = lax.rem(block, chunks) * RADIX_R + lax.div(block, chunks)
            for c0, (re, im) in enumerate(parts):
                both = jnp.concatenate([re, im], axis=1)
                inner[c0, place] = both.astype(inner.dtype)

        def fold(array):
            return jnp.sum(array.reshape(rows // 8, 8, N2), axis=0)

        acc[...] = jnp.zeros_like(acc)

        def start_block(block, carry):
            at = pl.ds(pl.multiple_of(block * rows, rows), rows)
            t_re = tmpl[block, 0].astype(jnp.float32)
            t_im = tmpl[block, 1].astype(jnp.float32)
            inverse = psd[block].astype(jnp.float32)
            x_re = spectrum[0, at]
            x_im = spectrum[1, at]
            p_re = x_re * t_re + x_im * t_im
            p_im = x_im * t_re - x_re * t_im
            heavy = inverse * inverse * (t_re * t_re + t_im * t_im)
            prod[0, at] = p_re
            prod[1, at] = p_im
            weight[at] = heavy
            acc[0] += fold(heavy)
            spread_out(block, p_re, p_im)
            return carry

        lax.fori_loop(0, freq, start_block, 0)
        variance = total(acc[0])

        def transforms(use):
            def pair(cp, carry):
                columns = [[] for _ in range(RADIX_R)]
                for half in range(2):
                    c0 = 2 * cp + half
                    left = inner[c0].reshape(N1, 2 * PART).astype(jnp.bfloat16)
                    lag = jnp.dot(left, stage_one[c0], preferred_element_type=jnp.float32)
                    found = [([], []) for _ in range(RADIX_R)]
                    for q in range(chunks):
                        y_re, y_im = [], []
                        for a in range(RADIX_R):
                            at = slice((q * RADIX_R + a) * rows, (q * RADIX_R + a + 1) * rows)
                            g = lag[at, :PART], lag[at, PART:]
                            at = slice(a * PART + q * rows, a * PART + (q + 1) * rows)
                            tw = twiddle[c0, at, :PART], twiddle[c0, at, PART:]
                            turned = times(g, tw)
                            y_re.append(turned[0])
                            y_im.append(turned[1])
                        for r0, (re, im) in enumerate(dft_four(y_re, y_im)):
                            found[r0][0].append(re)
                            found[r0][1].append(im)
                    for r0, (re, im) in enumerate(found):
                        columns[r0].append(jnp.concatenate([*re, *im], axis=0).astype(jnp.bfloat16))
                for r0 in range(RADIX_R):
                    right = jnp.concatenate(columns[r0], axis=1)
                    lag = jnp.dot(stage_two[r0], right, preferred_element_type=jnp.float32)
                    use(cp, r0, lag[:PART], lag[PART:])
                return carry

            lax.fori_loop(0, RADIX_C // 2, pair, 0, unroll=True)

        head_scale = 1.0 / (MODULUS * variance)

        def use_base(cp, r0, re, im):
            score[cp, r0] = (re * re + im * im) * head_scale

        transforms(use_base)

        acc[...] = jnp.zeros_like(acc)

        def moment_block(block, carry):
            at = pl.ds(pl.multiple_of(block * rows, rows), rows)
            heavy = weight[at]
            for j in range(CAL):
                acc[j] += fold(heavy * basis[j, block].astype(jnp.float32))
            return carry

        lax.fori_loop(0, freq, moment_block, 0)

        def response(j, carry):
            projection = total(acc[j]) / variance
            acc[CAL] = jnp.zeros_like(acc[CAL])

            def filter_block(block, inside):
                at = pl.ds(pl.multiple_of(block * rows, rows), rows)
                centred = basis[j, block].astype(jnp.float32) - projection
                acc[CAL] += fold(weight[at] * centred * centred)
                spread_out(block, prod[0, at] * centred, prod[1, at] * centred)
                return inside

            lax.fori_loop(0, freq, filter_block, 0)
            tail_scale = 1.0 / (MODULUS * total(acc[CAL]))

            def use_tail(cp, r0, re, im):
                score[cp, r0] += (re * re + im * im) * tail_scale

            transforms(use_tail)
            return carry

        lax.fori_loop(0, CAL, response, 0)
        for cp in range(RADIX_C // 2):
            for r0 in range(RADIX_R):
                done = score[cp, r0] * (1.0 / (DET * RESP))
                natural[2 * cp, pl.ds(r0, PART, stride=RADIX_R)] = done[:, :PART]
                natural[2 * cp + 1, pl.ds(r0, PART, stride=RADIX_R)] = done[:, PART:]
        left = jnp.concatenate([natural[c0].astype(jnp.bfloat16) for c0 in range(RADIX_C)], axis=1)
        span = N2 // planes
        whole = jnp.dot(left, unscramble[...], preferred_element_type=jnp.float32)
        for z in range(planes):
            blocks[z] = whole[:, z * span : (z + 1) * span]
        for o, ref in enumerate(outs):
            ref[...] = blocks[lax.rem(plane + o, planes)].astype(jnp.bfloat16)


def lag_scores(plan, rows, where, spectrum, tables, tmpl, small, own, other):
    vmem = pl.BlockSpec(memory_space=pltpu.VMEM)
    streams = [*tmpl, *small, *own, *other]
    inner_type = jnp.bfloat16 if rows % 16 == 0 else jnp.float32
    return pl.pallas_call(
        functools.partial(lag_kernel, plan, rows),
        out_shape=[jax.ShapeDtypeStruct((N1, N2 // plan.planes), jnp.bfloat16)] * plan.planes,
        in_specs=[pl.BlockSpec(memory_space=pltpu.SMEM), *[vmem] * (5 + len(streams))],
        out_specs=[vmem] * plan.planes,
        scratch_shapes=[
            pltpu.VMEM((plan.freq, 2, rows, N2), jnp.bfloat16),
            pltpu.VMEM((plan.freq, rows, N2), jnp.bfloat16),
            pltpu.VMEM((CAL, plan.freq, rows, N2), jnp.bfloat16),
            pltpu.VMEM((2, N1, N2), jnp.float32),
            pltpu.VMEM((N1, N2), jnp.float32),
            pltpu.VMEM((RADIX_C, plan.freq, rows, 2 * PART), inner_type),
            pltpu.VMEM((RADIX_C // 2, RADIX_R, PART, 2 * PART), jnp.float32),
            pltpu.VMEM((RADIX_C, N1, PART), jnp.float32),
            pltpu.VMEM((plan.planes, N1, N2 // plan.planes), jnp.float32),
            pltpu.VMEM((CAL + 1, 8, N2), jnp.float32),
        ],
        compiler_params=pltpu.CompilerParams(vmem_limit_bytes=(34 if rows % 16 == 0 else 58) * 1024 * 1024),
        name="lag_scores",
    )(where, spectrum, *tables, *streams)


def on_device(groups, strain, gate_start, psd_inverse, templates, basis):
    freq = lax.axis_size("freq")
    plan = Plan(freq, templates.shape[0], groups)
    me = lax.axis_index("freq")
    group = lax.axis_index("tmpl")
    plane, place = me // plan.width, me % plan.width
    cols, rows = strain.shape[1], psd_inverse.shape[1]

    packed = jnp.concatenate([strain[:, : cols // 2], strain[:, cols // 2 :]], axis=2)
    half = lax.dynamic_slice_in_dim(basis, 2 * (group % 2), 2, 1)
    inverse = psd_inverse.astype(jnp.bfloat16)
    shares = jnp.concatenate([packed[:, None], inverse[:, None], half], axis=1)
    piece = scatter_planes(plan, plane, shares)

    tmpl = scatter_templates(plan, place, templates)
    rings = gather_templates(plan, tmpl)

    small = gather_plane(plan, piece[:, :2])
    partner = [(g, g ^ 1) for g in range(groups)]
    own = gather_plane(plan, piece[:, 2:])
    other = [lax.ppermute(half, "tmpl", partner) for half in own[:-1]]
    last = lax.ppermute(jnp.concatenate(other), "freq", plan.swap(plan.bits[-1]))
    other.append(last)

    where = jnp.stack([plane, place]).astype(jnp.int32)
    zero = jnp.int32(0)
    stage_one, coarse, fine = column_tables(zero)
    table_r = row_table(zero)
    stage_two = lag_tables(zero)
    spectrum, twiddle, unscramble = spectrum_of(
        plan, rows, where, gate_start, table_r, stage_one, coarse, fine, small
    )
    scores = lag_scores(
        plan,
        rows,
        where,
        spectrum,
        (stage_one, stage_two, twiddle, unscramble),
        rings,
        small,
        own,
        other,
    )

    summed = scores[0].astype(jnp.float32)
    for o in range(1, plan.planes):
        got = lax.ppermute(scores[o], "freq", plan.shift_out(o))
        summed = summed + got.astype(jnp.float32)
    best = summed.astype(jnp.bfloat16)
    for b in plan.bits:
        side = (place // b) % 2
        span = best.shape[1] // 2
        send = lax.dynamic_slice_in_dim(best, (1 - side) * span, span, 1)
        keep = lax.dynamic_slice_in_dim(best, side * span, span, 1)
        best = jnp.maximum(keep, lax.ppermute(send, "freq", plan.swap(b)))
    b = groups // 2
    while b:
        side = (group // b) % 2
        span = best.shape[0] // 2
        send = lax.dynamic_slice_in_dim(best, (1 - side) * span, span, 0)
        keep = lax.dynamic_slice_in_dim(best, side * span, span, 0)
        swap = [(g, g ^ b) for g in range(groups)]
        best = jnp.maximum(keep, lax.ppermute(send, "tmpl", swap))
        b //= 2
    return best.astype(jnp.float32)


def solution(mesh):
    def whole(*args):
        return on_device(mesh.shape["tmpl"], *args)

    placed = (
        P(None, "freq", None),
        P(),
        P(None, "freq", None),
        P("tmpl", None, "freq", None),
        P(None, None, "freq", None),
    )
    return jax.shard_map(
        whole, mesh=mesh, in_specs=placed, out_specs=P("tmpl", "freq"), check_vma=False
    )
```

```python
import functools
import math

import jax
import jax.numpy as jnp
from jax import lax
from jax.experimental import pallas as pl
from jax.experimental.pallas import tpu as pltpu
from jax.sharding import PartitionSpec as P


N1 = 512
N2 = 1024
DET = 3
CAL = 4
RESP = 5
GATE_LEN = 4096
MODULUS = N1 * N2
RADIX_C = 8
RADIX_R = 4
PART = 128
HALF_ROOT = math.sqrt(0.5)


def phase(products, length):
    angles = (products % length).astype(jnp.float32) * (2.0 * math.pi / length)
    return jnp.cos(angles), jnp.sin(angles)


def times(left, right):
    return left[0] * right[0] - left[1] * right[1], left[0] * right[1] + left[1] * right[0]


def product_phase(rows, cols, length):
    fine = jnp.arange(32, dtype=jnp.int32)
    coarse = 32 * jnp.arange(rows // 32, dtype=jnp.int32)
    high = phase(coarse[:, None] * cols, length)
    low = phase(fine[:, None] * cols, length)
    real, imag = times([h[:, None] for h in high], [w[None] for w in low])
    return real.reshape(rows, -1), imag.reshape(rows, -1)


def iota(count):
    return jnp.arange(count, dtype=jnp.int32)


def row_table(zero):
    cos_r, sin_r = product_phase(N1, zero + iota(N1)[None], N1)
    return jnp.concatenate([cos_r, -sin_r], axis=0).astype(jnp.bfloat16)


def block_table(real, imag, transposed):
    up, low = (-imag, imag) if transposed else (imag, -imag)
    top = jnp.concatenate([real, up], axis=2)
    return jnp.concatenate([top, jnp.concatenate([low, real], axis=2)], axis=1).astype(jnp.bfloat16)


def lag_columns(zero):
    return zero + iota(RADIX_C)[:, None] + RADIX_C * iota(PART)[None, :]


def column_tables(zero):
    cols = lag_columns(zero)
    stage_one = block_table(*phase(iota(PART)[None, :, None] * cols[:, None, :], N2), False)
    coarse = 32 * iota(N1 // 32)
    high = phase(coarse[None, :, None] * cols[:, None, :], MODULUS)
    low = phase(iota(32)[None, :, None] * cols[:, None, :], MODULUS)
    return stage_one, jnp.stack(high), jnp.stack(low)


def lag_tables(zero):
    rows = zero + iota(RADIX_R)[:, None] + RADIX_R * iota(PART)[None, :]
    stage_two = block_table(*phase(rows[:, :, None] * iota(PART)[None, None, :], N1), True)
    return stage_two


class Plan:
    def __init__(self, freq, templates, groups):
        self.freq, self.width, self.groups = freq, templates, groups
        self.planes = freq // templates
        self.bits = [1 << b for b in reversed(range(templates.bit_length() - 1))]
        self.offsets = [0]
        for b in self.bits:
            self.offsets = self.offsets + [o ^ b for o in self.offsets]

    def swap(self, bit):
        return [(f, f ^ bit) for f in range(self.freq)]

    def devices(self, pairs):
        w = self.width
        return [(a * w + k, b * w + k) for a, b in pairs for k in range(w)]

    def shift_in(self, o):
        n = self.planes
        return self.devices([(z, (z + o) % n) for z in range(n) if (z + o) % n < DET])

    def shift_out(self, o):
        n = self.planes
        return self.devices([(z, (z + o) % n) for z in range(DET)])

    def back(self):
        n = self.planes
        return self.devices([(z, (z - 1) % n) for z in range(n)])


def pick(array, index, axis=0):
    return lax.dynamic_index_in_dim(array, index, axis, keepdims=False)


def scatter_planes(plan, plane, array):
    got = [pick(array, jnp.minimum(plane, DET - 1))]
    for o in range(1, plan.planes):
        send = pick(array, jnp.minimum((plane + o) % plan.planes, DET - 1))
        got.append(lax.ppermute(send, "freq", plan.shift_in(o)))
    return jnp.stack(got)


def spread_plane(plan, piece):
    held = piece[None]
    pieces = [held]
    for i, b in enumerate(plan.bits[:-1]):
        got = lax.ppermute(held, "freq", plan.swap(b))
        pieces.append(got)
        held = jnp.concatenate(pieces) if i + 2 < len(plan.bits) else None
    return pieces


def swap_last(plan, pieces):
    swap = plan.swap(plan.bits[-1])
    return [lax.ppermute(p, "freq", swap) for p in pieces]


def scatter_templates(plan, place, templates):
    held = templates[None]
    for b in plan.bits:
        mine = (place // b) % 2
        halves = held.reshape((held.shape[0], 2, held.shape[1] // 2) + held.shape[2:])
        got = lax.ppermute(pick(halves, 1 - mine, 1), "freq", plan.swap(b))
        held = jnp.concatenate([pick(halves, mine, 1), got])
    return held[:, 0]


def gather_templates(plan, piece):
    pieces = [piece]
    for _ in range(1, plan.planes):
        pieces.append(lax.ppermute(pieces[-1], "freq", plan.back()))
    return pieces


def dft_eight(real, imag):
    def add(a, b):
        return real_imag[a][0] + real_imag[b][0], real_imag[a][1] + real_imag[b][1]

    def sub(a, b):
        return real_imag[a][0] - real_imag[b][0], real_imag[a][1] - real_imag[b][1]

    real_imag = list(zip(real, imag))
    a0, a1 = add(0, 4), sub(0, 4)
    a2, a3 = add(2, 6), sub(2, 6)
    a4, a5 = add(1, 5), sub(1, 5)
    a6, a7 = add(3, 7), sub(3, 7)
    e0 = (a0[0] + a2[0], a0[1] + a2[1])
    e1 = (a0[0] - a2[0], a0[1] - a2[1])
    o0 = (a4[0] + a6[0], a4[1] + a6[1])
    o1 = (a4[0] - a6[0], a4[1] - a6[1])
    f0 = (a1[0] - a3[1], a1[1] + a3[0])
    f1 = (a1[0] + a3[1], a1[1] - a3[0])
    m = (HALF_ROOT * (a5[0] - a7[0]), HALF_ROOT * (a5[1] - a7[1]))
    n = (HALF_ROOT * (a5[0] + a7[0]), HALF_ROOT * (a5[1] + a7[1]))
    g0 = (m[0] - n[1], m[1] + n[0])
    g1 = (-m[0] - n[1], n[0] - m[1])
    return [
        (e0[0] + o0[0], e0[1] + o0[1]),
        (f0[0] + g0[0], f0[1] + g0[1]),
        (e1[0] - o1[1], e1[1] + o1[0]),
        (f1[0] + g1[0], f1[1] + g1[1]),
        (e0[0] - o0[0], e0[1] - o0[1]),
        (f0[0] - g0[0], f0[1] - g0[1]),
        (e1[0] + o1[1], e1[1] - o1[0]),
        (f1[0] - g1[0], f1[1] - g1[1]),
    ]


def dft_four(real, imag):
    s0, s1 = (real[0] + real[2], imag[0] + imag[2]), (real[0] - real[2], imag[0] - imag[2])
    t0, t1 = (real[1] + real[3], imag[1] + imag[3]), (real[1] - real[3], imag[1] - imag[3])
    return [
        (s0[0] + t0[0], s0[1] + t0[1]),
        (s1[0] - t1[1], s1[1] + t1[0]),
        (s0[0] - t0[0], s0[1] - t0[1]),
        (s1[0] + t1[1], s1[1] - t1[0]),
    ]


def from_plane_gather(plan, plane, place, pieces, put):
    m = 0
    for piece in pieces:
        for i in range(piece.shape[0]):
            for o in range(plan.planes):
                behind = lax.rem(plane - o + plan.planes, plan.planes)
                put(piece.at[i, o], behind * plan.width + (place ^ plan.offsets[m]))
            m += 1


def spectrum_kernel(
    plan, rows, where_ref, gates_ref, row_table_ref, stage_one, coarse_ref, fine_ref, *rest
):
    pieces, rest = rest[:-7], rest[-7:]
    out, twiddle, unscramble, blocks, samples, parts, sem = rest
    plane, place = where_ref[0], where_ref[1]

    @pl.when(plane < DET)
    def _():
        from_plane_gather(
            plan,
            plane,
            place,
            pieces,
            lambda src, f: pltpu.make_async_copy(src, blocks.at[f], sem).start(),
        )

        def twiddle_of(c0, carry):
            fine_re, fine_im = fine_ref[0, c0], fine_ref[1, c0]
            span = fine_re.shape[0]
            for a in range(N1 // span):
                high = coarse_ref[0, c0, a : a + 1], coarse_ref[1, c0, a : a + 1]
                re, im = times(high, (fine_re, fine_im))
                twiddle[c0, a * span : (a + 1) * span, :PART] = re
                twiddle[c0, a * span : (a + 1) * span, PART:] = im
            return carry

        lax.fori_loop(0, RADIX_C, twiddle_of, 0)
        row = lax.broadcasted_iota(jnp.int32, (PART, N2), 0)
        column = lax.broadcasted_iota(jnp.int32, (PART, N2), 1)
        for c0 in range(RADIX_C):
            hit = column == c0 + RADIX_C * row
            unscramble[c0 * PART : (c0 + 1) * PART] = jnp.where(hit, 1.0, 0.0).astype(jnp.bfloat16)
        pltpu.make_async_copy(blocks, blocks, sem).wait()
        tiles = N1 // PART

        starts = [gates_ref[plane, g] for g in range(gates_ref.shape[1])]
        step = lax.broadcasted_iota(jnp.int32, (rows, PART), 0)
        step = step + N2 * lax.broadcasted_iota(jnp.int32, (rows, PART), 1)

        def spread(block, carry):
            piece = blocks[block, 0].astype(jnp.float32)
            for half in range(2):
                at = pl.ds(pl.multiple_of((2 * block + half) * rows, rows), rows)
                for t in range(tiles):
                    first = half * N1 + t * PART
                    values = piece[:, first : first + PART]
                    for start in starts:
                        past = step + ((2 * block + half) * rows + t * PART * N2 - start)
                        values = jnp.where((past >= 0) & (past < GATE_LEN), 0.0, values)
                    samples[t, at] = values
            return carry

        lax.fori_loop(0, plan.freq, spread, 0)
        for first in range(0, RADIX_C, 2):
            right = []
            for a in (first, first + 1):
                found = [samples[t, pl.ds(a, PART, stride=RADIX_C)] for t in range(tiles)]
                right.append(jnp.concatenate([r.astype(jnp.bfloat16) for r in found], axis=1))
            section = lax.dot_general(
                row_table_ref[...],
                jnp.concatenate(right, axis=0),
                (((1,), (1,)), ((), ())),
                preferred_element_type=jnp.float32,
            )
            for a in (first, first + 1):
                lanes = slice((a - first) * PART, (a - first + 1) * PART)
                re, im = section[:N1, lanes], section[N1:, lanes]
                tw_re, tw_im = twiddle[a, :, :PART], twiddle[a, :, PART:]
                both = [re * tw_re + im * tw_im, im * tw_re - re * tw_im]
                both = jnp.concatenate(both, axis=1).astype(jnp.bfloat16)
                parts[a] = lax.dot_general(
                    both, stage_one[a], (((1,), (1,)), ((), ())), preferred_element_type=jnp.float32
                )

        def finish(block, carry):
            at = pl.ds(pl.multiple_of(block * rows, rows), rows)
            inverse = blocks[block, 1].astype(jnp.float32)
            re = [parts[a, at, :PART] for a in range(RADIX_C)]
            im = [parts[a, at, PART:] for a in range(RADIX_C)]
            for q, (y_im, y_re) in enumerate(dft_eight(im, re)):
                tile = slice(q * PART, (q + 1) * PART)
                out[0, at, tile] = y_re * inverse[:, tile]
                out[1, at, tile] = y_im * inverse[:, tile]
            return carry

        lax.fori_loop(0, plan.freq, finish, 0)


def spectrum_of(plan, rows, where, gates, table_r, stage_one, coarse, fine, pieces):
    vmem = pl.BlockSpec(memory_space=pltpu.VMEM)
    hbm = pl.BlockSpec(memory_space=pl.ANY)
    return pl.pallas_call(
        functools.partial(spectrum_kernel, plan, rows),
        out_shape=[
            jax.ShapeDtypeStruct((2, N1, N2), jnp.float32),
            jax.ShapeDtypeStruct((RADIX_C, N1, 2 * PART), jnp.float32),
            jax.ShapeDtypeStruct((N2, N2), jnp.bfloat16),
        ],
        in_specs=[*[pl.BlockSpec(memory_space=pltpu.SMEM)] * 2, *[vmem] * 4, *[hbm] * len(pieces)],
        out_specs=[vmem] * 3,
        scratch_shapes=[
            pltpu.VMEM((plan.freq, 2, rows, N2), jnp.bfloat16),
            pltpu.VMEM((N1 // PART, N2, PART), jnp.float32),
            pltpu.VMEM((RADIX_C, N1, 2 * PART), jnp.float32),
            pltpu.SemaphoreType.DMA,
        ],
        compiler_params=pltpu.CompilerParams(vmem_limit_bytes=(26 if rows % 16 == 0 else 40) * 1024 * 1024),
        name="spectrum",
    )(where, gates, table_r, stage_one, coarse, fine, *pieces)


def total(array):
    return jnp.sum(jnp.sum(array, axis=0, keepdims=True), axis=1, keepdims=True)


def lag_kernel(
    plan, rows, where_ref, spectrum, stage_one, stage_two, twiddle, unscramble, *rest
):
    n_tmpl = plan.planes
    tmpl_in, rest = rest[:n_tmpl], rest[n_tmpl:]
    small_in, rest = rest[:4], rest[4:]
    own_in, rest = rest[:4], rest[4:]
    near_in, rest = rest[:2], rest[2:]
    far_in, rest = rest[:4], rest[4:]
    outs, rest = rest[: plan.planes], rest[plan.planes :]
    tmpl, psd, basis, prod, weight, inner, score, natural, blocks, acc = rest
    plane, place = where_ref[0], where_ref[1]
    freq, width, planes = plan.freq, plan.width, plan.planes

    @pl.when(plane >= DET)
    def _():
        for ref in outs:
            ref[...] = jnp.zeros_like(ref)

    @pl.when(plane < DET)
    def _():
        for ahead, ref in enumerate(tmpl_in):
            source = lax.rem(plane + ahead, planes) * width
            for m in range(width):
                tmpl[source + (place ^ plan.offsets[m])] = ref[m]

        def put(target, select):
            def store(piece, f):
                target[f] = select(piece)

            return store

        from_pieces = functools.partial(from_plane_gather, plan, plane, place)
        from_pieces(small_in, put(psd, lambda p: p[1]))
        for j in range(2):
            from_pieces(own_in, put(basis.at[j], lambda p, j=j: p[j]))
            others = [near_in[0].at[:, :, pl.ds(j, 1)], far_in[j]]
            others += [near_in[1].at[:, :, pl.ds(j, 1)], far_in[2 + j]]
            from_pieces(others, put(basis.at[2 + j], lambda p: p[0]))

        chunks = PART // rows

        def spread_out(block, real, imag):
            tiles = [slice(a * PART, (a + 1) * PART) for a in range(RADIX_C)]
            parts = dft_eight([real[:, t] for t in tiles], [imag[:, t] for t in tiles])
            place = lax.rem(block, chunks) * RADIX_R + lax.div(block, chunks)
            for c0, (re, im) in enumerate(parts):
                both = jnp.concatenate([re, im], axis=1)
                inner[c0, place] = both.astype(inner.dtype)

        def fold(array):
            return jnp.sum(array.reshape(rows // 8, 8, N2), axis=0)

        acc[...] = jnp.zeros_like(acc)

        def start_block(block, carry):
            at = pl.ds(pl.multiple_of(block * rows, rows), rows)
            t_re = tmpl[block, 0].astype(jnp.float32)
            t_im = tmpl[block, 1].astype(jnp.float32)
            inverse = psd[block].astype(jnp.float32)
            x_re = spectrum[0, at]
            x_im = spectrum[1, at]
            p_re = x_re * t_re + x_im * t_im
            p_im = x_im * t_re - x_re * t_im
            heavy = inverse * inverse * (t_re * t_re + t_im * t_im)
            prod[0, at] = p_re
            prod[1, at] = p_im
            weight[at] = heavy
            acc[0] += fold(heavy)
            spread_out(block, p_re, p_im)
            return carry

        lax.fori_loop(0, freq, start_block, 0)
        variance = total(acc[0])

        def transforms(use):
            def pair(cp, carry):
                columns = [[] for _ in range(RADIX_R)]
                for half in range(2):
                    c0 = 2 * cp + half
                    left = inner[c0].reshape(N1, 2 * PART).astype(jnp.bfloat16)
                    lag = jnp.dot(left, stage_one[c0], preferred_element_type=jnp.float32)
                    found = [([], []) for _ in range(RADIX_R)]
                    for q in range(chunks):
                        y_re, y_im = [], []
                        for a in range(RADIX_R):
                            at = slice((q * RADIX_R + a) * rows, (q * RADIX_R + a + 1) * rows)
                            g = lag[at, :PART], lag[at, PART:]
                            at = slice(a * PART + q * rows, a * PART + (q + 1) * rows)
                            tw = twiddle[c0, at, :PART], twiddle[c0, at, PART:]
                            turned = times(g, tw)
                            y_re.append(turned[0])
                            y_im.append(turned[1])
                        for r0, (re, im) in enumerate(dft_four(y_re, y_im)):
                            found[r0][0].append(re)
                            found[r0][1].append(im)
                    for r0, (re, im) in enumerate(found):
                        columns[r0].append(jnp.concatenate([*re, *im], axis=0).astype(jnp.bfloat16))
                for r0 in range(RADIX_R):
                    right = jnp.concatenate(columns[r0], axis=1)
                    lag = jnp.dot(stage_two[r0], right, preferred_element_type=jnp.float32)
                    use(cp, r0, lag[:PART], lag[PART:])
                return carry

            lax.fori_loop(0, RADIX_C // 2, pair, 0, unroll=True)

        head_scale = 1.0 / (MODULUS * variance)

        def use_base(cp, r0, re, im):
            score[cp, r0] = (re * re + im * im) * head_scale

        transforms(use_base)

        acc[...] = jnp.zeros_like(acc)

        def moment_block(block, carry):
            at = pl.ds(pl.multiple_of(block * rows, rows), rows)
            heavy = weight[at]
            for j in range(CAL):
                acc[j] += fold(heavy * basis[j, block].astype(jnp.float32))
            return carry

        lax.fori_loop(0, freq, moment_block, 0)

        def response(j, carry):
            projection = total(acc[j]) / variance
            acc[CAL] = jnp.zeros_like(acc[CAL])

            def filter_block(block, inside):
                at = pl.ds(pl.multiple_of(block * rows, rows), rows)
                centred = basis[j, block].astype(jnp.float32) - projection
                acc[CAL] += fold(weight[at] * centred * centred)
                spread_out(block, prod[0, at] * centred, prod[1, at] * centred)
                return inside

            lax.fori_loop(0, freq, filter_block, 0)
            tail_scale = 1.0 / (MODULUS * total(acc[CAL]))

            def use_tail(cp, r0, re, im):
                score[cp, r0] += (re * re + im * im) * tail_scale

            transforms(use_tail)
            return carry

        lax.fori_loop(0, CAL, response, 0)
        for cp in range(RADIX_C // 2):
            for r0 in range(RADIX_R):
                done = score[cp, r0] * (1.0 / (DET * RESP))
                natural[2 * cp, pl.ds(r0, PART, stride=RADIX_R)] = done[:, :PART]
                natural[2 * cp + 1, pl.ds(r0, PART, stride=RADIX_R)] = done[:, PART:]
        left = jnp.concatenate([natural[c0].astype(jnp.bfloat16) for c0 in range(RADIX_C)], axis=1)
        span = N2 // planes
        whole = jnp.dot(left, unscramble[...], preferred_element_type=jnp.float32)
        for z in range(planes):
            blocks[z] = whole[:, z * span : (z + 1) * span]
        for o, ref in enumerate(outs):
            ref[...] = blocks[lax.rem(plane + o, planes)].astype(jnp.bfloat16)


def lag_scores(plan, rows, where, spectrum, tables, tmpl, small, own, near, far):
    vmem = pl.BlockSpec(memory_space=pltpu.VMEM)
    streams = [*tmpl, *small, *own, *near, *far]
    inner_type = jnp.bfloat16 if rows % 16 == 0 else jnp.float32
    return pl.pallas_call(
        functools.partial(lag_kernel, plan, rows),
        out_shape=[jax.ShapeDtypeStruct((N1, N2 // plan.planes), jnp.bfloat16)] * plan.planes,
        in_specs=[pl.BlockSpec(memory_space=pltpu.SMEM), *[vmem] * (5 + len(streams))],
        out_specs=[vmem] * plan.planes,
        scratch_shapes=[
            pltpu.VMEM((plan.freq, 2, rows, N2), jnp.bfloat16),
            pltpu.VMEM((plan.freq, rows, N2), jnp.bfloat16),
            pltpu.VMEM((CAL, plan.freq, rows, N2), jnp.bfloat16),
            pltpu.VMEM((2, N1, N2), jnp.float32),
            pltpu.VMEM((N1, N2), jnp.float32),
            pltpu.VMEM((RADIX_C, plan.freq, rows, 2 * PART), inner_type),
            pltpu.VMEM((RADIX_C // 2, RADIX_R, PART, 2 * PART), jnp.float32),
            pltpu.VMEM((RADIX_C, N1, PART), jnp.float32),
            pltpu.VMEM((plan.planes, N1, N2 // plan.planes), jnp.float32),
            pltpu.VMEM((CAL + 1, 8, N2), jnp.float32),
        ],
        compiler_params=pltpu.CompilerParams(vmem_limit_bytes=(34 if rows % 16 == 0 else 58) * 1024 * 1024),
        name="lag_scores",
    )(where, spectrum, *tables, *streams)


def on_device(groups, strain, gate_start, psd_inverse, templates, basis):
    freq = lax.axis_size("freq")
    plan = Plan(freq, templates.shape[0], groups)
    me = lax.axis_index("freq")
    group = lax.axis_index("tmpl")
    plane, place = me // plan.width, me % plan.width
    cols, rows = strain.shape[1], psd_inverse.shape[1]

    packed = jnp.concatenate([strain[:, : cols // 2], strain[:, cols // 2 :]], axis=2)
    half = lax.dynamic_slice_in_dim(basis, 2 * (group % 2), 2, 1)
    inverse = psd_inverse.astype(jnp.bfloat16)
    shares = jnp.concatenate([packed[:, None], inverse[:, None], half], axis=1)
    piece = scatter_planes(plan, plane, shares)

    tmpl = scatter_templates(plan, place, templates)
    rings = gather_templates(plan, tmpl)

    small = spread_plane(plan, piece[:, :2])
    small = small + swap_last(plan, small)
    partner = [(g, g ^ 1) for g in range(groups)]
    own = spread_plane(plan, piece[:, 2:])
    near = [lax.ppermute(own[0], "tmpl", partner)]
    far = [
        lax.ppermute(near[0][:, :, :1], "freq", plan.swap(plan.bits[0])),
        lax.ppermute(own[1][:, :, 1:], "tmpl", partner),
    ]
    own = own + swap_last(plan, own)
    near = near + swap_last(plan, near)
    far = far + swap_last(plan, far)

    where = jnp.stack([plane, place]).astype(jnp.int32)
    zero = jnp.int32(0)
    stage_one, coarse, fine = column_tables(zero)
    table_r = row_table(zero)
    stage_two = lag_tables(zero)
    spectrum, twiddle, unscramble = spectrum_of(
        plan, rows, where, gate_start, table_r, stage_one, coarse, fine, small
    )
    scores = lag_scores(
        plan,
        rows,
        where,
        spectrum,
        (stage_one, stage_two, twiddle, unscramble),
        rings,
        small,
        own,
        near,
        far,
    )

    summed = scores[0].astype(jnp.float32)
    for o in range(1, plan.planes):
        got = lax.ppermute(scores[o], "freq", plan.shift_out(o))
        summed = summed + got.astype(jnp.float32)
    best = summed.astype(jnp.bfloat16)
    for b in plan.bits:
        side = (place // b) % 2
        span = best.shape[1] // 2
        send = lax.dynamic_slice_in_dim(best, (1 - side) * span, span, 1)
        keep = lax.dynamic_slice_in_dim(best, side * span, span, 1)
        best = jnp.maximum(keep, lax.ppermute(send, "freq", plan.swap(b)))
    b = groups // 2
    while b:
        side = (group // b) % 2
        span = best.shape[0] // 2
        send = lax.dynamic_slice_in_dim(best, (1 - side) * span, span, 0)
        keep = lax.dynamic_slice_in_dim(best, side * span, span, 0)
        swap = [(g, g ^ b) for g in range(groups)]
        best = jnp.maximum(keep, lax.ppermute(send, "tmpl", swap))
        b //= 2
    return best.astype(jnp.float32)


def solution(mesh):
    def whole(*args):
        return on_device(mesh.shape["tmpl"], *args)

    placed = (
        P(None, "freq", None),
        P(),
        P(None, "freq", None),
        P("tmpl", None, "freq", None),
        P(None, None, "freq", None),
    )
    return jax.shard_map(
        whole, mesh=mesh, in_specs=placed, out_specs=P("tmpl", "freq"), check_vma=False
    )
```

```python
import functools
import math

import jax
import jax.numpy as jnp
from jax import lax
from jax.experimental import pallas as pl
from jax.experimental.pallas import tpu as pltpu
from jax.sharding import PartitionSpec as P


N1 = 512
N2 = 1024
DET = 3
CAL = 4
RESP = 5
GATE_LEN = 4096
MODULUS = N1 * N2
RADIX_C = 8
RADIX_R = 4
PART = 128
HALF_ROOT = math.sqrt(0.5)


def phase(products, length):
    angles = (products % length).astype(jnp.float32) * (2.0 * math.pi / length)
    return jnp.cos(angles), jnp.sin(angles)


def times(left, right):
    return left[0] * right[0] - left[1] * right[1], left[0] * right[1] + left[1] * right[0]


def product_phase(rows, cols, length):
    fine = jnp.arange(32, dtype=jnp.int32)
    coarse = 32 * jnp.arange(rows // 32, dtype=jnp.int32)
    high = phase(coarse[:, None] * cols, length)
    low = phase(fine[:, None] * cols, length)
    real, imag = times([h[:, None] for h in high], [w[None] for w in low])
    return real.reshape(rows, -1), imag.reshape(rows, -1)


def iota(count):
    return jnp.arange(count, dtype=jnp.int32)


def row_table(zero):
    cos_r, sin_r = product_phase(N1, zero + iota(N1)[None], N1)
    return jnp.concatenate([cos_r, -sin_r], axis=0).astype(jnp.bfloat16)


def block_table(real, imag, transposed):
    up, low = (-imag, imag) if transposed else (imag, -imag)
    top = jnp.concatenate([real, up], axis=2)
    return jnp.concatenate([top, jnp.concatenate([low, real], axis=2)], axis=1).astype(jnp.bfloat16)


def lag_columns(zero):
    return zero + iota(RADIX_C)[:, None] + RADIX_C * iota(PART)[None, :]


def column_tables(zero):
    cols = lag_columns(zero)
    stage_one = block_table(*phase(iota(PART)[None, :, None] * cols[:, None, :], N2), False)
    coarse = 32 * iota(N1 // 32)
    high = phase(coarse[None, :, None] * cols[:, None, :], MODULUS)
    low = phase(iota(32)[None, :, None] * cols[:, None, :], MODULUS)
    return stage_one, jnp.stack(high), jnp.stack(low)


def lag_tables(zero):
    rows = zero + iota(RADIX_R)[:, None] + RADIX_R * iota(PART)[None, :]
    stage_two = block_table(*phase(rows[:, :, None] * iota(PART)[None, None, :], N1), True)
    return stage_two


class Plan:
    def __init__(self, freq, templates, groups):
        self.freq, self.width, self.groups = freq, templates, groups
        self.planes = freq // templates
        self.bits = [1 << b for b in reversed(range(templates.bit_length() - 1))]
        self.offsets = [0]
        for b in self.bits:
            self.offsets = self.offsets + [o ^ b for o in self.offsets]

    def swap(self, bit):
        return [(f, f ^ bit) for f in range(self.freq)]

    def devices(self, pairs):
        w = self.width
        return [(a * w + k, b * w + k) for a, b in pairs for k in range(w)]

    def shift_in(self, o):
        n = self.planes
        return self.devices([(z, (z + o) % n) for z in range(n) if (z + o) % n < DET])

    def shift_out(self, o):
        n = self.planes
        return self.devices([(z, (z + o) % n) for z in range(DET)])

    def back(self):
        n = self.planes
        return self.devices([(z, (z - 1) % n) for z in range(n)])


def pick(array, index, axis=0):
    return lax.dynamic_index_in_dim(array, index, axis, keepdims=False)


def scatter_planes(plan, plane, array):
    got = [pick(array, jnp.minimum(plane, DET - 1))]
    for o in range(1, plan.planes):
        send = pick(array, jnp.minimum((plane + o) % plan.planes, DET - 1))
        got.append(lax.ppermute(send, "freq", plan.shift_in(o)))
    return jnp.stack(got)


def spread_plane(plan, piece):
    held = piece[None]
    pieces = [held]
    for i, b in enumerate(plan.bits[:-1]):
        got = lax.ppermute(held, "freq", plan.swap(b))
        pieces.append(got)
        held = jnp.concatenate(pieces) if i + 2 < len(plan.bits) else None
    return pieces


def swap_last(plan, pieces):
    swap = plan.swap(plan.bits[-1])
    return [lax.ppermute(p, "freq", swap) for p in pieces]


def scatter_templates(plan, place, templates):
    held = templates[None]
    for b in plan.bits:
        mine = (place // b) % 2
        halves = held.reshape((held.shape[0], 2, held.shape[1] // 2) + held.shape[2:])
        got = lax.ppermute(pick(halves, 1 - mine, 1), "freq", plan.swap(b))
        held = jnp.concatenate([pick(halves, mine, 1), got])
    return held[:, 0]


def gather_templates(plan, piece):
    pieces = [piece]
    for _ in range(1, plan.planes):
        pieces.append(lax.ppermute(pieces[-1], "freq", plan.back()))
    return pieces


def dft_eight(real, imag):
    def add(a, b):
        return real_imag[a][0] + real_imag[b][0], real_imag[a][1] + real_imag[b][1]

    def sub(a, b):
        return real_imag[a][0] - real_imag[b][0], real_imag[a][1] - real_imag[b][1]

    real_imag = list(zip(real, imag))
    a0, a1 = add(0, 4), sub(0, 4)
    a2, a3 = add(2, 6), sub(2, 6)
    a4, a5 = add(1, 5), sub(1, 5)
    a6, a7 = add(3, 7), sub(3, 7)
    e0 = (a0[0] + a2[0], a0[1] + a2[1])
    e1 = (a0[0] - a2[0], a0[1] - a2[1])
    o0 = (a4[0] + a6[0], a4[1] + a6[1])
    o1 = (a4[0] - a6[0], a4[1] - a6[1])
    f0 = (a1[0] - a3[1], a1[1] + a3[0])
    f1 = (a1[0] + a3[1], a1[1] - a3[0])
    m = (HALF_ROOT * (a5[0] - a7[0]), HALF_ROOT * (a5[1] - a7[1]))
    n = (HALF_ROOT * (a5[0] + a7[0]), HALF_ROOT * (a5[1] + a7[1]))
    g0 = (m[0] - n[1], m[1] + n[0])
    g1 = (-m[0] - n[1], n[0] - m[1])
    return [
        (e0[0] + o0[0], e0[1] + o0[1]),
        (f0[0] + g0[0], f0[1] + g0[1]),
        (e1[0] - o1[1], e1[1] + o1[0]),
        (f1[0] + g1[0], f1[1] + g1[1]),
        (e0[0] - o0[0], e0[1] - o0[1]),
        (f0[0] - g0[0], f0[1] - g0[1]),
        (e1[0] + o1[1], e1[1] - o1[0]),
        (f1[0] - g1[0], f1[1] - g1[1]),
    ]


def dft_four(real, imag):
    s0, s1 = (real[0] + real[2], imag[0] + imag[2]), (real[0] - real[2], imag[0] - imag[2])
    t0, t1 = (real[1] + real[3], imag[1] + imag[3]), (real[1] - real[3], imag[1] - imag[3])
    return [
        (s0[0] + t0[0], s0[1] + t0[1]),
        (s1[0] - t1[1], s1[1] + t1[0]),
        (s0[0] - t0[0], s0[1] - t0[1]),
        (s1[0] + t1[1], s1[1] - t1[0]),
    ]


def from_plane_gather(plan, plane, place, pieces, put):
    m = 0
    for piece in pieces:
        for i in range(piece.shape[0]):
            for o in range(plan.planes):
                behind = lax.rem(plane - o + plan.planes, plan.planes)
                put(piece.at[i, o], behind * plan.width + (place ^ plan.offsets[m]))
            m += 1


def spectrum_kernel(
    plan, rows, where_ref, gates_ref, row_table_ref, stage_one, coarse_ref, fine_ref, *rest
):
    pieces, rest = rest[:-7], rest[-7:]
    out, twiddle, unscramble, blocks, samples, parts, sem = rest
    plane, place = where_ref[0], where_ref[1]

    @pl.when(plane < DET)
    def _():
        from_plane_gather(
            plan,
            plane,
            place,
            pieces,
            lambda src, f: pltpu.make_async_copy(src, blocks.at[f], sem).start(),
        )

        def twiddle_of(c0, carry):
            fine_re, fine_im = fine_ref[0, c0], fine_ref[1, c0]
            span = fine_re.shape[0]
            for a in range(N1 // span):
                high = coarse_ref[0, c0, a : a + 1], coarse_ref[1, c0, a : a + 1]
                re, im = times(high, (fine_re, fine_im))
                twiddle[c0, a * span : (a + 1) * span, :PART] = re
                twiddle[c0, a * span : (a + 1) * span, PART:] = im
            return carry

        lax.fori_loop(0, RADIX_C, twiddle_of, 0)
        row = lax.broadcasted_iota(jnp.int32, (PART, N2), 0)
        column = lax.broadcasted_iota(jnp.int32, (PART, N2), 1)
        for c0 in range(RADIX_C):
            hit = column == c0 + RADIX_C * row
            unscramble[c0 * PART : (c0 + 1) * PART] = jnp.where(hit, 1.0, 0.0).astype(jnp.bfloat16)
        pltpu.make_async_copy(blocks, blocks, sem).wait()
        tiles = N1 // PART

        starts = [gates_ref[plane, g] for g in range(gates_ref.shape[1])]
        step = lax.broadcasted_iota(jnp.int32, (rows, PART), 0)
        step = step + N2 * lax.broadcasted_iota(jnp.int32, (rows, PART), 1)

        def spread(block, carry):
            piece = blocks[block, 0].astype(jnp.float32)
            for half in range(2):
                at = pl.ds(pl.multiple_of((2 * block + half) * rows, rows), rows)
                for t in range(tiles):
                    first = half * N1 + t * PART
                    values = piece[:, first : first + PART]
                    for start in starts:
                        past = step + ((2 * block + half) * rows + t * PART * N2 - start)
                        values = jnp.where((past >= 0) & (past < GATE_LEN), 0.0, values)
                    samples[t, at] = values
            return carry

        lax.fori_loop(0, plan.freq, spread, 0)
        for first in range(0, RADIX_C, 2):
            right = []
            for a in (first, first + 1):
                found = [samples[t, pl.ds(a, PART, stride=RADIX_C)] for t in range(tiles)]
                right.append(jnp.concatenate([r.astype(jnp.bfloat16) for r in found], axis=1))
            section = lax.dot_general(
                row_table_ref[...],
                jnp.concatenate(right, axis=0),
                (((1,), (1,)), ((), ())),
                preferred_element_type=jnp.float32,
            )
            for a in (first, first + 1):
                lanes = slice((a - first) * PART, (a - first + 1) * PART)
                re, im = section[:N1, lanes], section[N1:, lanes]
                tw_re, tw_im = twiddle[a, :, :PART], twiddle[a, :, PART:]
                both = [re * tw_re + im * tw_im, im * tw_re - re * tw_im]
                both = jnp.concatenate(both, axis=1).astype(jnp.bfloat16)
                parts[a] = lax.dot_general(
                    both, stage_one[a], (((1,), (1,)), ((), ())), preferred_element_type=jnp.float32
                )

        def finish(block, carry):
            at = pl.ds(pl.multiple_of(block * rows, rows), rows)
            inverse = blocks[block, 1].astype(jnp.float32)
            re = [parts[a, at, :PART] for a in range(RADIX_C)]
            im = [parts[a, at, PART:] for a in range(RADIX_C)]
            for q, (y_im, y_re) in enumerate(dft_eight(im, re)):
                tile = slice(q * PART, (q + 1) * PART)
                out[0, at, tile] = y_re * inverse[:, tile]
                out[1, at, tile] = y_im * inverse[:, tile]
            return carry

        lax.fori_loop(0, plan.freq, finish, 0)


def spectrum_of(plan, rows, where, gates, table_r, stage_one, coarse, fine, pieces):
    vmem = pl.BlockSpec(memory_space=pltpu.VMEM)
    hbm = pl.BlockSpec(memory_space=pl.ANY)
    return pl.pallas_call(
        functools.partial(spectrum_kernel, plan, rows),
        out_shape=[
            jax.ShapeDtypeStruct((2, N1, N2), jnp.float32),
            jax.ShapeDtypeStruct((RADIX_C, N1, 2 * PART), jnp.float32),
            jax.ShapeDtypeStruct((N2, N2), jnp.bfloat16),
        ],
        in_specs=[*[pl.BlockSpec(memory_space=pltpu.SMEM)] * 2, *[vmem] * 4, *[hbm] * len(pieces)],
        out_specs=[vmem] * 3,
        scratch_shapes=[
            pltpu.VMEM((plan.freq, 2, rows, N2), jnp.bfloat16),
            pltpu.VMEM((N1 // PART, N2, PART), jnp.float32),
            pltpu.VMEM((RADIX_C, N1, 2 * PART), jnp.float32),
            pltpu.SemaphoreType.DMA,
        ],
        compiler_params=pltpu.CompilerParams(vmem_limit_bytes=(26 if rows % 16 == 0 else 40) * 1024 * 1024),
        name="spectrum",
    )(where, gates, table_r, stage_one, coarse, fine, *pieces)


def total(array):
    return jnp.sum(jnp.sum(array, axis=0, keepdims=True), axis=1, keepdims=True)


def lag_kernel(
    plan, rows, where_ref, spectrum, stage_one, stage_two, twiddle, unscramble, *rest
):
    n_tmpl = plan.planes
    tmpl_in, rest = rest[:n_tmpl], rest[n_tmpl:]
    small_in, rest = rest[:4], rest[4:]
    own_in, rest = rest[:4], rest[4:]
    near_in, rest = rest[:2], rest[2:]
    far_in, rest = rest[:4], rest[4:]
    outs, rest = rest[: plan.planes], rest[plan.planes :]
    tmpl, psd, basis, prod, weight, inner, score, natural, blocks, acc = rest
    plane, place = where_ref[0], where_ref[1]
    freq, width, planes = plan.freq, plan.width, plan.planes

    @pl.when(plane >= DET)
    def _():
        for ref in outs:
            ref[...] = jnp.zeros_like(ref)

    @pl.when(plane < DET)
    def _():
        for ahead, ref in enumerate(tmpl_in):
            source = lax.rem(plane + ahead, planes) * width
            for m in range(width):
                tmpl[source + (place ^ plan.offsets[m])] = ref[m]

        def put(target, select):
            def store(piece, f):
                target[f] = select(piece)

            return store

        from_pieces = functools.partial(from_plane_gather, plan, plane, place)
        from_pieces(small_in, put(psd, lambda p: p[1]))
        for j in range(2):
            from_pieces(own_in, put(basis.at[j], lambda p, j=j: p[j]))
            others = [near_in[0].at[:, :, pl.ds(j, 1)], far_in[j]]
            others += [near_in[1].at[:, :, pl.ds(j, 1)], far_in[2 + j]]
            from_pieces(others, put(basis.at[2 + j], lambda p: p[0]))

        chunks = PART // rows

        def spread_out(block, real, imag):
            tiles = [slice(a * PART, (a + 1) * PART) for a in range(RADIX_C)]
            parts = dft_eight([real[:, t] for t in tiles], [imag[:, t] for t in tiles])
            place = lax.rem(block, chunks) * RADIX_R + lax.div(block, chunks)
            for c0, (re, im) in enumerate(parts):
                both = jnp.concatenate([re, im], axis=1)
                inner[c0, place] = both.astype(inner.dtype)

        def fold(array):
            return jnp.sum(array.reshape(rows // 8, 8, N2), axis=0)

        acc[...] = jnp.zeros_like(acc)

        def start_block(block, carry):
            at = pl.ds(pl.multiple_of(block * rows, rows), rows)
            t_re = tmpl[block, 0].astype(jnp.float32)
            t_im = tmpl[block, 1].astype(jnp.float32)
            inverse = psd[block].astype(jnp.float32)
            x_re = spectrum[0, at]
            x_im = spectrum[1, at]
            p_re = x_re * t_re + x_im * t_im
            p_im = x_im * t_re - x_re * t_im
            heavy = inverse * inverse * (t_re * t_re + t_im * t_im)
            prod[0, at] = p_re
            prod[1, at] = p_im
            weight[at] = heavy
            acc[0] += fold(heavy)
            spread_out(block, p_re, p_im)
            return carry

        lax.fori_loop(0, freq, start_block, 0)
        variance = total(acc[0])

        def transforms(use):
            def first_stage(c0):
                left = inner[c0].reshape(N1, 2 * PART).astype(jnp.bfloat16)
                return jnp.dot(left, stage_one[c0], preferred_element_type=jnp.float32)

            ahead = [first_stage(0), first_stage(1)]
            for cp in range(RADIX_C // 2):
                lags = ahead
                if 2 * cp + 2 < RADIX_C:
                    ahead = [first_stage(2 * cp + 2), first_stage(2 * cp + 3)]
                columns = [[] for _ in range(RADIX_R)]
                for half in range(2):
                    c0 = 2 * cp + half
                    lag = lags[half]
                    found = [([], []) for _ in range(RADIX_R)]
                    for q in range(chunks):
                        y_re, y_im = [], []
                        for a in range(RADIX_R):
                            at = slice((q * RADIX_R + a) * rows, (q * RADIX_R + a + 1) * rows)
                            g = lag[at, :PART], lag[at, PART:]
                            at = slice(a * PART + q * rows, a * PART + (q + 1) * rows)
                            tw = twiddle[c0, at, :PART], twiddle[c0, at, PART:]
                            turned = times(g, tw)
                            y_re.append(turned[0])
                            y_im.append(turned[1])
                        for r0, (re, im) in enumerate(dft_four(y_re, y_im)):
                            found[r0][0].append(re)
                            found[r0][1].append(im)
                    for r0, (re, im) in enumerate(found):
                        columns[r0].append(jnp.concatenate([*re, *im], axis=0).astype(jnp.bfloat16))
                for r0 in range(RADIX_R):
                    right = jnp.concatenate(columns[r0], axis=1)
                    lag = jnp.dot(stage_two[r0], right, preferred_element_type=jnp.float32)
                    use(cp, r0, lag[:PART], lag[PART:])

        head_scale = 1.0 / (MODULUS * variance)

        def use_base(cp, r0, re, im):
            score[cp, r0] = (re * re + im * im) * head_scale

        transforms(use_base)

        acc[...] = jnp.zeros_like(acc)

        def moment_block(block, carry):
            at = pl.ds(pl.multiple_of(block * rows, rows), rows)
            heavy = weight[at]
            for j in range(CAL):
                acc[j] += fold(heavy * basis[j, block].astype(jnp.float32))
            return carry

        lax.fori_loop(0, freq, moment_block, 0)

        def response(j, carry):
            projection = total(acc[j]) / variance
            acc[CAL] = jnp.zeros_like(acc[CAL])

            def filter_block(block, inside):
                at = pl.ds(pl.multiple_of(block * rows, rows), rows)
                centred = basis[j, block].astype(jnp.float32) - projection
                acc[CAL] += fold(weight[at] * centred * centred)
                spread_out(block, prod[0, at] * centred, prod[1, at] * centred)
                return inside

            lax.fori_loop(0, freq, filter_block, 0)
            tail_scale = 1.0 / (MODULUS * total(acc[CAL]))

            def use_tail(cp, r0, re, im):
                score[cp, r0] += (re * re + im * im) * tail_scale

            transforms(use_tail)
            return carry

        lax.fori_loop(0, CAL, response, 0)
        for cp in range(RADIX_C // 2):
            for r0 in range(RADIX_R):
                done = score[cp, r0] * (1.0 / (DET * RESP))
                natural[2 * cp, pl.ds(r0, PART, stride=RADIX_R)] = done[:, :PART]
                natural[2 * cp + 1, pl.ds(r0, PART, stride=RADIX_R)] = done[:, PART:]
        left = jnp.concatenate([natural[c0].astype(jnp.bfloat16) for c0 in range(RADIX_C)], axis=1)
        span = N2 // planes
        whole = jnp.dot(left, unscramble[...], preferred_element_type=jnp.float32)
        for z in range(planes):
            blocks[z] = whole[:, z * span : (z + 1) * span]
        for o, ref in enumerate(outs):
            ref[...] = blocks[lax.rem(plane + o, planes)].astype(jnp.bfloat16)


def lag_scores(plan, rows, where, spectrum, tables, tmpl, small, own, near, far):
    vmem = pl.BlockSpec(memory_space=pltpu.VMEM)
    streams = [*tmpl, *small, *own, *near, *far]
    inner_type = jnp.bfloat16 if rows % 16 == 0 else jnp.float32
    return pl.pallas_call(
        functools.partial(lag_kernel, plan, rows),
        out_shape=[jax.ShapeDtypeStruct((N1, N2 // plan.planes), jnp.bfloat16)] * plan.planes,
        in_specs=[pl.BlockSpec(memory_space=pltpu.SMEM), *[vmem] * (5 + len(streams))],
        out_specs=[vmem] * plan.planes,
        scratch_shapes=[
            pltpu.VMEM((plan.freq, 2, rows, N2), jnp.bfloat16),
            pltpu.VMEM((plan.freq, rows, N2), jnp.bfloat16),
            pltpu.VMEM((CAL, plan.freq, rows, N2), jnp.bfloat16),
            pltpu.VMEM((2, N1, N2), jnp.float32),
            pltpu.VMEM((N1, N2), jnp.float32),
            pltpu.VMEM((RADIX_C, plan.freq, rows, 2 * PART), inner_type),
            pltpu.VMEM((RADIX_C // 2, RADIX_R, PART, 2 * PART), jnp.float32),
            pltpu.VMEM((RADIX_C, N1, PART), jnp.float32),
            pltpu.VMEM((plan.planes, N1, N2 // plan.planes), jnp.float32),
            pltpu.VMEM((CAL + 1, 8, N2), jnp.float32),
        ],
        compiler_params=pltpu.CompilerParams(vmem_limit_bytes=(30 if rows % 16 == 0 else 58) * 1024 * 1024),
        name="lag_scores",
    )(where, spectrum, *tables, *streams)


def on_device(groups, strain, gate_start, psd_inverse, templates, basis):
    freq = lax.axis_size("freq")
    plan = Plan(freq, templates.shape[0], groups)
    me = lax.axis_index("freq")
    group = lax.axis_index("tmpl")
    plane, place = me // plan.width, me % plan.width
    cols, rows = strain.shape[1], psd_inverse.shape[1]

    packed = jnp.concatenate([strain[:, : cols // 2], strain[:, cols // 2 :]], axis=2)
    half = lax.dynamic_slice_in_dim(basis, 2 * (group % 2), 2, 1)
    inverse = psd_inverse.astype(jnp.bfloat16)
    shares = jnp.concatenate([packed[:, None], inverse[:, None], half], axis=1)
    piece = scatter_planes(plan, plane, shares)

    tmpl = scatter_templates(plan, place, templates)
    rings = gather_templates(plan, tmpl)

    small = spread_plane(plan, piece[:, :2])
    small = small + swap_last(plan, small)
    partner = [(g, g ^ 1) for g in range(groups)]
    own = spread_plane(plan, piece[:, 2:])
    near = [lax.ppermute(own[0], "tmpl", partner)]
    far = [
        lax.ppermute(near[0][:, :, :1], "freq", plan.swap(plan.bits[0])),
        lax.ppermute(own[1][:, :, 1:], "tmpl", partner),
    ]
    own = own + swap_last(plan, own)
    near = near + swap_last(plan, near)
    far = far + swap_last(plan, far)

    where = jnp.stack([plane, place]).astype(jnp.int32)
    zero = jnp.int32(0)
    stage_one, coarse, fine = column_tables(zero)
    table_r = row_table(zero)
    stage_two = lag_tables(zero)
    spectrum, twiddle, unscramble = spectrum_of(
        plan, rows, where, gate_start, table_r, stage_one, coarse, fine, small
    )
    scores = lag_scores(
        plan,
        rows,
        where,
        spectrum,
        (stage_one, stage_two, twiddle, unscramble),
        rings,
        small,
        own,
        near,
        far,
    )

    summed = scores[0].astype(jnp.float32)
    for o in range(1, plan.planes):
        got = lax.ppermute(scores[o], "freq", plan.shift_out(o))
        summed = summed + got.astype(jnp.float32)
    best = summed.astype(jnp.bfloat16)
    for b in plan.bits:
        side = (place // b) % 2
        span = best.shape[1] // 2
        send = lax.dynamic_slice_in_dim(best, (1 - side) * span, span, 1)
        keep = lax.dynamic_slice_in_dim(best, side * span, span, 1)
        best = jnp.maximum(keep, lax.ppermute(send, "freq", plan.swap(b)))
    b = groups // 2
    while b:
        side = (group // b) % 2
        span = best.shape[0] // 2
        send = lax.dynamic_slice_in_dim(best, (1 - side) * span, span, 0)
        keep = lax.dynamic_slice_in_dim(best, side * span, span, 0)
        swap = [(g, g ^ b) for g in range(groups)]
        best = jnp.maximum(keep, lax.ppermute(send, "tmpl", swap))
        b //= 2
    return best.astype(jnp.float32)


def solution(mesh):
    def whole(*args):
        return on_device(mesh.shape["tmpl"], *args)

    placed = (
        P(None, "freq", None),
        P(),
        P(None, "freq", None),
        P("tmpl", None, "freq", None),
        P(None, None, "freq", None),
    )
    return jax.shard_map(
        whole, mesh=mesh, in_specs=placed, out_specs=P("tmpl", "freq"), check_vma=False
    )
```
